256 devices in a mesh: ctx: 32 (over y, x, z_hi), head: 8 (over z_lo, core).
Axes of the slice: x: 4, y: 4, z: 8 (z_hi: 2, z_lo: 4; z = z_hi * 4 + z_lo), core: 2. Of those that a mesh axis runs over, the one named last changes fastest.
Arguments:
- queries: bfloat16 [32768, 2048], P(('ctx', 'head')), may hold values from -5.5 to 5.5
- key_vecs: bfloat16 [32768, 2048], P(('ctx', 'head')), may hold values from -5.5 to 5.5
- value_vecs: bfloat16 [32768, 2048], P(('ctx', 'head')), may hold values from -6 to 6
- out_grads: bfloat16 [32768, 2048], P(('ctx', 'head')), may hold values from -6 to 6
- local_offsets: int32 [256, 4], P('ctx'), may hold values from 0 to 7, as said below
- partner_pool: int32 [32, 2, 5], replicated, may hold values from 0 to 7, as said below
- partner_picks: int32 [256, 2, 4], P('ctx'), may hold values from 0 to 4, as said below
Outputs:
- query_grads: bfloat16 [32768, 2048], P(('ctx', 'head'))
- key_grads: bfloat16 [32768, 2048], P(('ctx', 'head'))
- value_grads: bfloat16 [32768, 2048], P(('ctx', 'head'))
The draws below stay inside these ranges and needn't reach their ends.
Inputs may be any that keep to these rules, and one draw needn't show every extreme that they name: `local_offsets`: each row holds 4 distinct offsets. `partner_pool`: each row of 5 entries names distinct blocks. `partner_picks`: each row of 4 entries holds distinct positions.
All inputs are finite; a program needn't handle non-finite values.
Results may differ from the reference program's by a relative error of at most 0.0069.
Values may be sent and summed in bfloat16 or wider, within the bound.
A program may use at most 64 MiB of HBM per device.

```python
import jax
import jax.numpy as jnp
from jax import lax

H = 16
DH = 128
BLK = 128
BITS = 2
TOK_DEV = 128
TOKENS = 32768
NB = 8
NQB = 256
GROUPS = 32
LOCAL = 4
POOL = 5
GIVEN = 4
N_HEAD = 8


def distinct_rows(base_key, row_count, span_size, take_count):
    row_keys = jax.random.split(base_key, row_count)

    def shuffle_one(row_key):
        return jax.random.permutation(row_key, span_size).astype(jnp.int32)
    shuffled = jax.vmap(shuffle_one)(row_keys)
    top_pos = jnp.argmax(shuffled[0] == span_size - 1)
    shuffled = shuffled.at[0].set(jnp.roll(shuffled[0], -top_pos))
    if row_count > 1:
        low_pos = jnp.argmax(shuffled[1] == 0)
        shuffled = shuffled.at[1].set(jnp.roll(shuffled[1], -low_pos))
    return shuffled[:, :take_count]


def draw_queries(key, part):
    noise_key = jax.random.fold_in(key, 202)
    result = jnp.clip(1.5 * jax.random.normal(noise_key, (TOKENS, H * DH), jnp.float32), -5.5, 5.5)
    return result.astype(jnp.bfloat16)


def draw_key_vecs(key, part):
    noise_key = jax.random.fold_in(key, 303)
    result = jnp.clip(jax.random.normal(noise_key, (TOKENS, H * DH), jnp.float32), -5.5, 5.5)
    return result.astype(jnp.bfloat16)


def draw_local_offsets(key, part):
    folded = jax.random.fold_in(key, 404)
    return distinct_rows(folded, NQB, NB, LOCAL).astype(jnp.int32)


def draw_partner_pool(key, part):
    folded = jax.random.fold_in(key, 505)
    return distinct_rows(folded, GROUPS * BITS, NB, POOL).reshape(GROUPS, BITS, POOL)


def draw_partner_picks(key, part):
    folded = jax.random.fold_in(key, 606)
    return distinct_rows(folded, NQB * BITS, POOL, GIVEN).reshape(NQB, BITS, GIVEN)


def block_levels(own_key, shape, pieces, smallest, top_value):
    gain, own = 1.0, jax.random.fold_in(own_key, 6)
    for dim, parts in pieces:
        heights = jnp.exp(jax.random.uniform(jax.random.fold_in(own, dim), (parts,), jnp.float32, smallest / len(pieces), top_value / len(pieces)))
        gain = gain * jnp.repeat(heights, shape[dim] // parts).reshape([-1 if axis == dim else 1 for axis in range(len(shape))])
    return gain


def centred(own_key, extent, deviation, bound, pieces=(), kind=jnp.bfloat16):
    values = jax.random.normal(own_key, extent, jnp.float32) * deviation
    if len(pieces) > 0:
        values = block_levels(own_key, extent, pieces, -0.22, 0.18) * values
    return jnp.clip(values, min=-bound, max=bound).astype(kind)


def setup_inputs(seed: int = 0) -> dict:
    arg_keys = jax.random.split(jax.random.key(seed), 8)
    return {
        "queries": draw_queries(jax.random.fold_in(arg_keys[7], 71), 0),
        "key_vecs": draw_key_vecs(jax.random.fold_in(arg_keys[7], 71), 0),
        "value_vecs": centred(arg_keys[2], (TOKENS, H * DH), 1.0, 6.0, ((0, 256),)),
        "out_grads": centred(arg_keys[3], (TOKENS, H * DH), 1.0, 6.0, ((0, 256),)),
        "local_offsets": draw_local_offsets(jax.random.fold_in(arg_keys[7], 71), 0),
        "partner_pool": draw_partner_pool(jax.random.fold_in(arg_keys[7], 71), 0),
        "partner_picks": draw_partner_picks(jax.random.fold_in(arg_keys[7], 71), 0),
    }


def reference(queries, key_vecs, value_vecs, out_grads, local_offsets, partner_pool, partner_picks):
    blocks = TOK_DEV * N_HEAD // BLK
    block_total = TOKENS // BLK
    softmax_scale = DH ** -0.5
    query_f = queries.astype(jnp.float32).reshape(block_total, BLK, H, DH)
    key_f = key_vecs.astype(jnp.float32).reshape(block_total, BLK, H, DH)
    value_f = value_vecs.astype(jnp.float32).reshape(block_total, BLK, H, DH)
    grad_f = out_grads.astype(jnp.float32).reshape(block_total, BLK, H, DH)
    block_ids = jnp.arange(block_total, dtype=jnp.int32)
    groups = block_ids // blocks
    inner_idx = block_ids % blocks
    local_idx = groups[:, None] * blocks + (inner_idx[:, None] + local_offsets) % blocks
    bit_values = jnp.left_shift(jnp.int32(1), jnp.arange(BITS, dtype=jnp.int32))
    partners = jnp.bitwise_xor(groups[:, None], bit_values[None, :])
    pool_rows = partner_pool[groups]
    given_idx = jnp.take_along_axis(pool_rows, partner_picks, axis=2)
    remote_idx = partners[:, :, None] * blocks + given_idx
    key_index = jnp.concatenate([local_idx, remote_idx.reshape(block_total, -1)], axis=1).astype(jnp.int32)
    key_count = key_index.shape[1]

    def attend(carry_in, block_id):
        acc_key, acc_value = carry_in
        chosen = key_index[block_id]
        query_part = query_f[block_id]
        grad_part = grad_f[block_id]
        key_part = key_f[chosen].reshape(key_count * BLK, H, DH)
        value_part = value_f[chosen].reshape(key_count * BLK, H, DH)
        scores = jnp.einsum("qhd,khd->hqk", query_part, key_part) * softmax_scale
        row_max = jnp.max(scores, axis=-1, keepdims=True)
        exp_scores = jnp.exp(scores - row_max)
        weights = exp_scores / jnp.sum(exp_scores, axis=-1, keepdims=True)
        prob_grad = jnp.einsum("qhd,khd->hqk", grad_part, value_part)
        row_delta = jnp.sum(weights * prob_grad, axis=-1, keepdims=True)
        score_grad = lax.optimization_barrier((softmax_scale * weights * (prob_grad - row_delta)).astype(jnp.bfloat16)).astype(jnp.float32)
        weights_half = lax.optimization_barrier(weights.astype(jnp.bfloat16)).astype(jnp.float32)
        query_out = jnp.einsum("hqk,khd->qhd", score_grad, key_part)
        key_out = jnp.einsum("hqk,qhd->khd", score_grad, query_part)
        value_out = jnp.einsum("hqk,qhd->khd", weights_half, grad_part)
        acc_key = acc_key.at[chosen].add(key_out.reshape(key_count, BLK, H, DH))
        acc_value = acc_value.at[chosen].add(value_out.reshape(key_count, BLK, H, DH))
        return (acc_key, acc_value), query_out.astype(jnp.bfloat16)

    zeros_init = jnp.zeros((block_total, BLK, H, DH), jnp.float32)
    (acc_key, acc_value), query_rows = lax.scan(attend, (zeros_init, zeros_init), block_ids)
    query_grads = query_rows.reshape(TOKENS, H * DH)
    key_grads = acc_key.reshape(TOKENS, H * DH).astype(jnp.bfloat16)
    value_grads = acc_value.reshape(TOKENS, H * DH).astype(jnp.bfloat16)
    return query_grads, key_grads, value_grads
```

```python
import jax
import jax.numpy as jnp
from jax import lax
from jax.experimental import pallas as pl
from jax.experimental.pallas import tpu as pltpu
from jax.sharding import PartitionSpec as P

MESH = pl.DeviceIdType.MESH
DH = 128
BLK = 128
NKEY = 12
TILES = 18
ZERO = 16 * NKEY
SCALE = DH**-0.5
f32 = jnp.float32
bf16 = jnp.bfloat16
ORDER = [(dx, dz) for dz in (4, 3, 5, 2, 6, 1, 7, 0) for dx in (1, 0)]


def place():
    ctx = lax.axis_index("ctx")
    head = lax.axis_index("head")
    return ctx, (ctx // 2) % 2, (ctx % 2) * 4 + head // 2, head % 2


def device(ctx, xb, z, core):
    return ((ctx // 4) * 4 + xb * 2 + z // 4, (z % 4) * 2 + core)


def greet(ctx, targets, count):
    barrier = pltpu.get_barrier_semaphore()
    for cond, (xb, z, core) in targets:

        @pl.when(cond)
        def _(xb=xb, z=z, core=core):
            pl.semaphore_signal(
                barrier, 1, device_id=device(ctx, xb, z, core), device_id_type=MESH
            )

    pl.semaphore_wait(barrier, count)


def remote(src, dst, ssem, rsem, dev):
    return pltpu.make_async_remote_copy(
        src_ref=src, dst_ref=dst, send_sem=ssem, recv_sem=rsem, device_id=dev, device_id_type=MESH
    )


def scatter_kernel(q, k, v, g, meta, qd, kv, rmeta, ssem, rsem, fsem, msem):
    ctx, xb, z, core = place()
    qd[:, 0:128, 128:256] = jnp.zeros((16, 128, 128), bf16)
    qd[:, 128:256, 0:128] = jnp.zeros((16, 128, 128), bf16)
    away = core != xb
    others = []
    for s in range(8):
        zs = (z + s) % 8
        for c in range(2):
            cond = jnp.logical_or(away, jnp.logical_or(zs != z, core != c))
            others.append((cond, (core, zs, c)))
    others.append((away, (xb, z, 1 - core)))
    greet(ctx, others, 16)
    slot = z * 2 + core

    def dst(a):
        if a == 0:
            return kv.at[slot, :, 0:128]
        if a == 1:
            return kv.at[slot, :, 128:256]
        if a == 2:
            return qd.at[slot, 0:128, 0:128]
        return qd.at[slot, 128:256, 128:256]

    srcs = (k, v, q, g)
    for a0 in (0, 2):
        for o, (dx, dz) in enumerate(ORDER):
            xd, zd = xb ^ dx, (z + dz) % 8
            cols = pl.ds(pl.multiple_of((xd * 8 + zd) * 128, 128), 128)
            for a in (a0, a0 + 1):
                src = srcs[a].at[:, cols]
                rc = remote(src, dst(a), ssem.at[a, o], rsem.at[a, slot], device(ctx, xd, zd, xb))
                if (dx, dz) == (0, 0):

                    @pl.when(away)
                    def _(rc=rc):
                        rc.start()

                    @pl.when(jnp.logical_not(away))
                    def _(src=src, a=a):
                        pltpu.make_async_copy(src, dst(a), rsem.at[a, slot]).start()
                else:
                    rc.start()
    mine = (z % 4) * 2 + core
    mrow = z // 4
    for dx in (0, 1):
        rc = remote(
            meta, rmeta.at[mrow], msem.at[0, dx], msem.at[1, mrow], device(ctx, xb ^ dx, mine, xb)
        )
        if dx == 1:
            rc.start()
        else:
            here = jnp.logical_and(jnp.logical_not(away), mine == z)

            @pl.when(jnp.logical_not(here))
            def _(rc=rc):
                rc.start()

            @pl.when(here)
            def _():
                pltpu.make_async_copy(meta, rmeta.at[mrow], msem.at[1, mrow]).start()

    here_dev = device(ctx, xb, z, 1 - core)

    def arrived(a, n, ref):
        remote(ref, ref, ssem.at[a, 0], rsem.at[a, n], here_dev).wait_recv()

    for n in range(16):
        arrived(0, n, kv.at[n, :, 0:128])
        arrived(1, n, kv.at[n, :, 128:256])
    forward = remote(kv.at[0:16], kv.at[16:32], fsem.at[0], fsem.at[1], here_dev)
    forward.start()
    for n in range(16):
        arrived(2, n, qd.at[n, 0:128, 0:128])
        arrived(3, n, qd.at[n, 128:256, 128:256])
    forward.wait()
    for n in range(2):
        remote(meta, rmeta.at[n], msem.at[0, 0], msem.at[1, n], here_dev).wait_recv()
    for o, (dx, dz) in enumerate(ORDER):
        for a in range(4):
            src = srcs[a].at[:, 0:128]
            rc = remote(src, src, ssem.at[a, o], rsem.at[a, 0], here_dev)
            if (dx, dz) == (0, 0):

                @pl.when(away)
                def _(rc=rc):
                    rc.wait_send()
            else:
                rc.wait_send()
    remote(meta, meta, msem.at[0, 1], msem.at[1, 0], here_dev).wait_send()

    @pl.when(jnp.logical_not(here))
    def _():
        remote(meta, meta, msem.at[0, 0], msem.at[1, 0], here_dev).wait_send()


def dot_t(a, b):
    return lax.dot_general(a, b, (((1,), (1,)), ((), ())), preferred_element_type=f32)


def dot(a, b):
    return jnp.dot(a, b, preferred_element_type=f32)


def tables(rmeta, pool, group0, idx, slot):
    @pl.loop(0, 16)
    def _(n):
        u, i = n // 8, n % 8
        g = group0 + u
        loc = [(i + rmeta[u, i, j]) % 8 for j in range(4)]
        for j in range(4):
            idx[n * NKEY + j] = u * 8 + loc[j]
        for kb in range(8):
            s = jnp.int32(ZERO)
            for j in range(4):
                s = jnp.where(loc[j] == kb, n * NKEY + j, s)
            slot[n * TILES + kb] = s
        for b in range(2):
            base = (1 - u) * 8 if b == 0 else 16 + u * 8
            picks = [rmeta[u, i, 4 + b * 4 + t] for t in range(4)]
            for t in range(4):
                idx[n * NKEY + 4 + b * 4 + t] = base + pool[(g * 2 + b) * 5 + picks[t]]
            for p in range(5):
                s = jnp.int32(ZERO)
                for t in range(4):
                    s = jnp.where(picks[t] == p, n * NKEY + 4 + b * 4 + t, s)
                slot[n * TILES + 8 + b * 5 + p] = s


def pool_place(pool, group, b, kb, none):
    s = jnp.int32(none)
    for p in range(5):
        s = jnp.where(pool[(group * 2 + b) * 5 + p] == kb, p, s)
    return s


def attend_block(n, idx, qd, kv, kt, sp, x, dq):
    ids = [idx[n * NKEY + j] for j in range(NKEY)]
    sp[...] = dot_t(jnp.concatenate([kv[r] for r in ids], axis=0), qd[n])
    m = jnp.full((8, 128), -jnp.inf, f32)
    for j in range(NKEY):
        s = sp[j * 128 : (j + 1) * 128, 0:128].reshape(16, 8, 128)
        m = jnp.maximum(m, jnp.max(s, axis=0))
    m = jnp.max(m, axis=0, keepdims=True) * SCALE
    den = jnp.zeros((8, 128), f32)
    num = jnp.zeros((8, 128), f32)
    for j in range(NKEY):
        s = sp[j * 128 : (j + 1) * 128, 0:128]
        p = sp[j * 128 : (j + 1) * 128, 128:256]
        e = jnp.exp(s * SCALE - m)
        sp[j * 128 : (j + 1) * 128, 0:128] = e
        den = den + jnp.sum(e.reshape(16, 8, 128), axis=0)
        num = num + jnp.sum((e * p).reshape(16, 8, 128), axis=0)
    rden = 1.0 / jnp.sum(den, axis=0, keepdims=True)
    delta = jnp.sum(num, axis=0, keepdims=True) * rden
    rscaled = rden * SCALE
    for j in range(NKEY):
        e = sp[j * 128 : (j + 1) * 128, 0:128]
        p = sp[j * 128 : (j + 1) * 128, 128:256]
        x[n * NKEY + j, :, 128:256] = (e * rden).astype(bf16)
        x[n * NKEY + j, :, 0:128] = ((e * rscaled) * (p - delta)).astype(bf16)
    kts = jnp.concatenate([kt[r] for r in ids], axis=1)
    ds = jnp.concatenate([x[n * NKEY + j, :, 0:128] for j in range(NKEY)], axis=0)
    dq[n] = dot(kts, ds).T.astype(bf16)


def compute_kernel(rmeta, pool, qd, kv, dq, own, part, idx, slot, kt, x, sp, acc):
    ctx, xb, z, core = place()
    group0 = (ctx // 4) * 4 + core * 2
    tables(rmeta, pool, group0, idx, slot)
    x[ZERO] = jnp.zeros((128, 256), bf16)
    acc[26] = jnp.zeros((128, 256), f32)

    @pl.loop(0, 32)
    def _(b):
        kt[b] = kv[b, :, 0:128].T

    @pl.loop(0, 16)
    def _(n):
        attend_block(n, idx, qd, kv, kt, sp, x, dq)

    def tile_sum(u, t):
        rows = jnp.concatenate([x[slot[(u * 8 + i) * TILES + t]] for i in range(8)], axis=1)
        return dot(rows, qd[pl.ds(u * 8, 8)].reshape(2048, 256))

    for u in range(2):

        @pl.loop(0, 13)
        def _(t):
            acc[u * 13 + t] = tile_sum(u, t)

        @pl.loop(0, 5)
        def _(p):
            part[u * 5 + p] = tile_sum(u, 13 + p)

    for u in range(2):

        @pl.loop(0, 8)
        def _(kb):
            p = pool_place(pool, group0 + 1 - u, 0, kb, 18 - (1 - u) * 13)
            own[u * 8 + kb] = acc[u * 13 + kb] + acc[(1 - u) * 13 + 8 + p]


def gather_kernel(pool, dq, own, part, oq, ok, ov, recv, fin, ssem, rsem, psem):
    ctx, xb, z, core = place()
    group0 = (ctx // 4) * 4 + core * 2
    recv[10] = jnp.zeros((128, 256), f32)
    away = core != xb
    others = []
    for s in range(8):
        zs = (z + s) % 8
        for x in range(2):
            cond = jnp.logical_or(away, jnp.logical_or(zs != z, xb != x))
            others.append((cond, (x, zs, xb)))
    others.append((jnp.logical_not(away), (xb, z, 1 - core)))
    greet(ctx, others, jnp.where(away, 17, 15))
    here_dev = device(ctx, xb, z, 1 - core)
    swap = remote(part, recv.at[0:10], psem.at[0], psem.at[1], here_dev)
    swap.start()
    cols = pl.ds(pl.multiple_of((xb * 8 + z) * 128, 128), 128)
    order = [(dz, c) for dz in (4, 3, 5, 2, 6, 1, 7, 0) for c in (0, 1)]
    outs = (oq, ok, ov)
    sem_row = xb * 8 + z

    def src(a, n):
        if a == 0:
            return dq.at[n]
        return fin.at[n, :, (a - 1) * 128 : a * 128]

    def send(a, o):
        dz, c = order[o]
        zd = (z + dz) % 8
        n = zd * 2 + c
        dst = outs[a].at[:, cols]
        rc = remote(src(a, n), dst, ssem.at[a, o], rsem.at[a, sem_row], device(ctx, core, zd, c))
        if dz == 0:
            here = jnp.logical_and(jnp.logical_not(away), core == c)

            @pl.when(jnp.logical_not(here))
            def _():
                rc.start()

            @pl.when(here)
            def _():
                pltpu.make_async_copy(src(a, n), dst, rsem.at[a, sem_row]).start()
        else:
            rc.start()

    for o in range(16):
        send(0, o)
    swap.wait()
    for o in range(16):
        dz, c = order[o]
        n = ((z + dz) % 8) * 2 + c
        u = n // 8
        p = pool_place(pool, (ctx // 4) * 4 + (1 - core) * 2 + u, 1, n % 8, 10 - u * 5)
        fin[n] = (own[n] + recv[u * 5 + p]).astype(bf16)
        send(1, o)
        send(2, o)
    for a in range(3):
        for r in range(16):
            ref = outs[a].at[:, r * 128 : (r + 1) * 128]
            remote(ref, ref, ssem.at[a, 0], rsem.at[a, r], here_dev).wait_recv()
    for o in range(16):
        dz, c = order[o]
        for a in range(3):
            rc = remote(dq.at[0], dq.at[0], ssem.at[a, o], rsem.at[a, 0], here_dev)
            if dz == 0:

                @pl.when(jnp.logical_or(away, core != c))
                def _(rc=rc):
                    rc.wait_send()
            else:
                rc.wait_send()


def per_device(q, k, v, g, local_offsets, partner_pool, partner_picks):
    hbm = pl.BlockSpec(memory_space=pltpu.HBM)
    vm = pl.BlockSpec(memory_space=pltpu.VMEM)
    sm = pl.BlockSpec(memory_space=pltpu.SMEM)
    dma = pltpu.SemaphoreType.DMA
    meta = jnp.concatenate([local_offsets, partner_picks.reshape(8, 8)], axis=1)
    meta = jnp.pad(meta, ((0, 0), (0, 116)))
    pool = partner_pool.reshape(-1)
    sds = jax.ShapeDtypeStruct
    qd, kv, rmeta = pl.pallas_call(
        scatter_kernel,
        name="scatter",
        out_shape=(
            sds((16, 256, 256), bf16),
            sds((32, 128, 256), bf16),
            sds((2, 8, 128), jnp.int32),
        ),
        in_specs=[hbm] * 4 + [vm],
        out_specs=(vm, vm, vm),
        scratch_shapes=[dma((4, 16)), dma((4, 16)), dma((2,)), dma((2, 2))],
        compiler_params=pltpu.CompilerParams(collective_id=0, has_side_effects=True),
    )(q, k, v, g, meta)
    dq, own, part = pl.pallas_call(
        compute_kernel,
        name="compute",
        out_shape=(
            sds((16, 128, 128), bf16),
            sds((16, 128, 256), f32),
            sds((10, 128, 256), f32),
        ),
        in_specs=[sm, sm, vm, vm],
        out_specs=(vm, vm, vm),
        scratch_shapes=[
            pltpu.SMEM((16 * NKEY,), jnp.int32),
            pltpu.SMEM((16 * TILES,), jnp.int32),
            pltpu.VMEM((32, 128, 128), bf16),
            pltpu.VMEM((ZERO + 1, 128, 256), bf16),
            pltpu.VMEM((NKEY * 128, 256), f32),
            pltpu.VMEM((27, 128, 256), f32),
        ],
        compiler_params=pltpu.CompilerParams(vmem_limit_bytes=58 << 20),
    )(rmeta, pool, qd, kv)
    return pl.pallas_call(
        gather_kernel,
        name="gather",
        out_shape=tuple(sds((128, 2048), bf16) for _ in range(3)),
        in_specs=[sm, vm, vm, vm],
        out_specs=(hbm, hbm, hbm),
        scratch_shapes=[
            pltpu.VMEM((11, 128, 256), f32),
            pltpu.VMEM((16, 128, 256), bf16),
            dma((3, 16)),
            dma((3, 16)),
            dma((2,)),
        ],
        compiler_params=pltpu.CompilerParams(collective_id=1, has_side_effects=True),
    )(pool, dq, own, part)


def solution(mesh):
    tok = P(("ctx", "head"), None)
    return jax.shard_map(
        per_device,
        mesh=mesh,
        in_specs=(tok, tok, tok, tok, P("ctx", None), P(), P("ctx", None, None)),
        out_specs=(tok, tok, tok),
        check_vma=False,
    )
```

```python
import jax
import jax.numpy as jnp
from jax import lax
from jax.experimental import pallas as pl
from jax.experimental.pallas import tpu as pltpu
from jax.sharding import PartitionSpec as P

MESH = pl.DeviceIdType.MESH
DH = 128
BLK = 128
NKEY = 12
TILES = 18
ZERO = 16 * NKEY
SCALE = DH**-0.5
f32 = jnp.float32
bf16 = jnp.bfloat16
SHIFTS = (0, 1, 7, 2, 6, 3, 5, 4)
ORDER = [(dx, dz) for dz in SHIFTS for dx in (0, 1)]


def place():
    ctx = lax.axis_index("ctx")
    head = lax.axis_index("head")
    return ctx, (ctx // 2) % 2, (ctx % 2) * 4 + head // 2, head % 2


def device(ctx, xb, z, core):
    return ((ctx // 4) * 4 + xb * 2 + z // 4, (z % 4) * 2 + core)


def remote(src, dst, ssem, rsem, dev):
    return pltpu.make_async_remote_copy(
        src_ref=src, dst_ref=dst, send_sem=ssem, recv_sem=rsem, device_id=dev, device_id_type=MESH
    )


def dot_t(a, b):
    return lax.dot_general(a, b, (((1,), (1,)), ((), ())), preferred_element_type=f32)


def dot(a, b):
    return jnp.dot(a, b, preferred_element_type=f32)


def tables(offs, picks, pool, group0, idx, slot):
    @pl.loop(0, 16)
    def _(n):
        u, i = n // 8, n % 8
        g = group0 + u
        loc = [(i + offs[u, j, i]) % 8 for j in range(4)]
        for j in range(4):
            idx[n * NKEY + j] = u * 8 + loc[j]
        for kb in range(8):
            s = jnp.int32(ZERO)
            for j in range(4):
                s = jnp.where(loc[j] == kb, n * NKEY + j, s)
            slot[n * TILES + kb] = s
        for b in range(2):
            base = (1 - u) * 8 if b == 0 else 16 + u * 8
            picked = [picks[u, b, t, i] for t in range(4)]
            for t in range(4):
                idx[n * NKEY + 4 + b * 4 + t] = base + pool[picked[t], b, g]
            for p in range(5):
                s = jnp.int32(ZERO)
                for t in range(4):
                    s = jnp.where(picked[t] == p, n * NKEY + 4 + b * 4 + t, s)
                slot[n * TILES + 8 + b * 5 + p] = s


def pool_place(pool, group, b, kb, none):
    s = jnp.int32(none)
    for p in range(5):
        s = jnp.where(pool[p, b, group] == kb, p, s)
    return s


def attend_block(n, idx, qd, kv, kt, sp, x, dq):
    ids = [idx[n * NKEY + j] for j in range(NKEY)]
    sp[...] = dot_t(jnp.concatenate([kv[r] for r in ids], axis=0), qd[n])
    m = jnp.full((8, 128), -jnp.inf, f32)
    for j in range(NKEY):
        s = sp[j * 128 : (j + 1) * 128, 0:128].reshape(16, 8, 128)
        m = jnp.maximum(m, jnp.max(s, axis=0))
    m = jnp.max(m, axis=0, keepdims=True) * SCALE
    den = jnp.zeros((8, 128), f32)
    num = jnp.zeros((8, 128), f32)
    for j in range(NKEY):
        s = sp[j * 128 : (j + 1) * 128, 0:128]
        p = sp[j * 128 : (j + 1) * 128, 128:256]
        e = jnp.exp(s * SCALE - m)
        sp[j * 128 : (j + 1) * 128, 0:128] = e
        den = den + jnp.sum(e.reshape(16, 8, 128), axis=0)
        num = num + jnp.sum((e * p).reshape(16, 8, 128), axis=0)
    rden = 1.0 / jnp.sum(den, axis=0, keepdims=True)
    delta = jnp.sum(num, axis=0, keepdims=True) * rden
    rscaled = rden * SCALE
    for j in range(NKEY):
        e = sp[j * 128 : (j + 1) * 128, 0:128]
        p = sp[j * 128 : (j + 1) * 128, 128:256]
        x[n * NKEY + j, :, 128:256] = (e * rden).astype(bf16)
        x[n * NKEY + j, :, 0:128] = ((e * rscaled) * (p - delta)).astype(bf16)
    kts = jnp.concatenate([kt[r] for r in ids], axis=1)
    ds = jnp.concatenate([x[n * NKEY + j, :, 0:128] for j in range(NKEY)], axis=0)
    dq[n] = dot(kts, ds).T.astype(bf16)


def shift(o):
    return lax.rem(o, 2) * ((o + 1) // 2) + (1 - lax.rem(o, 2)) * lax.rem(8 - o // 2, 8)


def kernel(
    q, k, v, g, offsets, partner_picks, pool,
    oq, ok, ov,
    qd, kv, kt, x, sp0, sp1, dq, part, near, recv, fin,
    voffs, vpicks, offs, picks, idx, slot,
    ssem, rsem, fsem, msem, lsem, osem, orsem, psem,
):
    ctx, xb, z, core = place()
    group0 = (ctx // 4) * 4 + core * 2
    away = core != xb
    at_home = core == xb
    here_dev = device(ctx, xb, z, 1 - core)
    barrier = pltpu.get_barrier_semaphore()
    for dx in range(2):
        for dz in SHIFTS:
            for dc in range(2):
                if (dx, dz, dc) != (0, 0, 0):
                    dev = device(ctx, xb ^ dx, (z + dz) % 8, core ^ dc)
                    pl.semaphore_signal(barrier, 1, device_id=dev, device_id_type=MESH)
    qd[:, 0:128, 128:256] = jnp.zeros((16, 128, 128), bf16)
    qd[:, 128:256, 0:128] = jnp.zeros((16, 128, 128), bf16)
    pl.semaphore_wait(barrier, 31)

    mine = (z % 4) * 2 + core
    mrow = z // 4
    small = ((offsets, voffs, offs), (partner_picks, vpicks, picks))
    meta_here = jnp.logical_and(at_home, mine == z)
    for dx in (0, 1):
        for b, (src, dst, _) in enumerate(small):
            rc = remote(
                src, dst.at[mrow], msem.at[b, dx], msem.at[b, 2 + mrow],
                device(ctx, xb ^ dx, mine, xb),
            )
            if dx == 1:
                rc.start()
            else:

                @pl.when(jnp.logical_not(meta_here))
                def _(rc=rc):
                    rc.start()

                @pl.when(meta_here)
                def _(src=src, dst=dst, b=b):
                    pltpu.make_async_copy(src, dst.at[mrow], msem.at[b, 2 + mrow]).start()

    slot_here = z * 2 + core
    srcs = (k, v, q, g)

    def place_of(a, n):
        if a == 0:
            return kv.at[n, :, 0:128]
        if a == 1:
            return kv.at[n, :, 128:256]
        if a == 2:
            return qd.at[n, 0:128, 0:128]
        return qd.at[n, 128:256, 128:256]

    for a0 in (0, 2):
        for o, (dx, dz) in enumerate(ORDER):
            xd, zd = xb ^ dx, (z + dz) % 8
            cols = pl.ds(pl.multiple_of((xd * 8 + zd) * 128, 128), 128)
            for a in (a0, a0 + 1):
                src = srcs[a].at[:, cols]
                dst = place_of(a, slot_here)
                rc = remote(
                    src, dst, ssem.at[a, o], rsem.at[a, slot_here], device(ctx, xd, zd, xb)
                )
                if (dx, dz) == (0, 0):

                    @pl.when(away)
                    def _(rc=rc):
                        rc.start()

                    @pl.when(at_home)
                    def _(src=src, dst=dst, a=a):
                        pltpu.make_async_copy(src, dst, rsem.at[a, slot_here]).start()
                else:
                    rc.start()

    def arrived(a, n):
        ref = place_of(a, n)
        remote(ref, ref, ssem.at[a, 0], rsem.at[a, n], here_dev).wait_recv()

    for n in range(2):
        for b, (src, dst, _) in enumerate(small):
            remote(src, dst.at[n], msem.at[b, 0], msem.at[b, 2 + n], here_dev).wait_recv()
    for b, (_, src, dst) in enumerate(small):
        local = pltpu.make_async_copy(src, dst, lsem.at[b])
        local.start()
        local.wait()
    tables(offs, picks, pool, group0, idx, slot)
    x[ZERO] = jnp.zeros((128, 256), bf16)
    near[10] = jnp.zeros((128, 256), f32)
    recv[10] = jnp.zeros((128, 256), f32)

    def forward(n):
        return remote(kv.at[n], kv.at[16 + n], fsem.at[0, n], fsem.at[1, n], here_dev)

    @pl.loop(0, 8)
    def _(o):
        zs = (z + 8 - shift(o)) % 8
        for c in range(2):
            n = zs * 2 + c
            arrived(0, n)
            arrived(1, n)
            forward(n).start()
            kt[n] = kv[n, :, 0:128].T

    @pl.loop(0, 8)
    def _(o):
        zs = (z + 8 - shift(o)) % 8
        for c in range(2):
            n = zs * 2 + c
            forward(n).wait_recv()
            kt[16 + n] = kv[16 + n, :, 0:128].T

    cols = pl.ds(pl.multiple_of((xb * 8 + z) * 128, 128), 128)
    row = xb * 8 + z
    outs = (oq, ok, ov)

    def result(a, n):
        if a == 0:
            return dq.at[n]
        return fin.at[n, :, (a - 1) * 128 : a * 128]

    def out_copy(a, n, zs, c):
        return remote(
            result(a, n), outs[a].at[:, cols], osem.at[a, n], orsem.at[a, row],
            device(ctx, core, zs, c),
        )

    def stays(zs, c):
        return jnp.logical_and(at_home, jnp.logical_and(zs == z, core == c))

    def send(a, n, zs, c):
        @pl.when(jnp.logical_not(stays(zs, c)))
        def _():
            out_copy(a, n, zs, c).start()

        @pl.when(stays(zs, c))
        def _():
            pltpu.make_async_copy(result(a, n), outs[a].at[:, cols], orsem.at[a, row]).start()

    @pl.loop(0, 8)
    def _(o):
        zs = (z + 8 - shift(o)) % 8
        for c in range(2):
            arrived(2, zs * 2 + c)
            arrived(3, zs * 2 + c)
        for c, sp in ((0, sp0), (1, sp1)):
            attend_block(zs * 2 + c, idx, qd, kv, kt, sp, x, dq)
        for c in range(2):
            send(0, zs * 2 + c, zs, c)

    def tile_sum(u, t):
        rows = jnp.concatenate([x[slot[(u * 8 + i) * TILES + t]] for i in range(8)], axis=1)
        return dot(rows, qd[pl.ds(u * 8, 8)].reshape(2048, 256))

    @pl.loop(0, 10)
    def _(t):
        part[t] = tile_sum(t // 5, 13 + t % 5)

    swap = remote(part, recv.at[0:10], psem.at[0], psem.at[1], here_dev)
    swap.start()

    @pl.loop(0, 10)
    def _(t):
        near[t] = tile_sum(t // 5, 8 + t % 5)

    swap.wait()

    @pl.loop(0, 8)
    def _(o):
        zs = (z + 8 - shift(o)) % 8
        u = zs // 4
        for c in range(2):
            n = zs * 2 + c
            p = (1 - u) * 5 + pool_place(pool, group0 + 1 - u, 0, n % 8, 10 - (1 - u) * 5)
            r = u * 5 + pool_place(
                pool, (ctx // 4) * 4 + (1 - core) * 2 + u, 1, n % 8, 10 - u * 5
            )
            fin[n] = (tile_sum(u, n % 8) + near[p] + recv[r]).astype(bf16)
            send(1, n, zs, c)
            send(2, n, zs, c)

    @pl.loop(0, 16)
    def _(r):
        for a in range(3):
            ref = outs[a].at[:, pl.ds(pl.multiple_of(r * 128, 128), 128)]
            remote(ref, ref, osem.at[a, 0], orsem.at[a, r], here_dev).wait_recv()

    for o, (dx, dz) in enumerate(ORDER):
        for a in range(4):
            src = srcs[a].at[:, 0:128]
            rc = remote(src, src, ssem.at[a, o], rsem.at[a, 0], here_dev)
            if (dx, dz) == (0, 0):

                @pl.when(away)
                def _(rc=rc):
                    rc.wait_send()
            else:
                rc.wait_send()
    for b, (src, dst, _) in enumerate(small):
        remote(src, dst.at[0], msem.at[b, 1], msem.at[b, 2], here_dev).wait_send()

        @pl.when(jnp.logical_not(meta_here))
        def _(src=src, dst=dst, b=b):
            remote(src, dst.at[0], msem.at[b, 0], msem.at[b, 2], here_dev).wait_send()

    @pl.loop(0, 8)
    def _(zs):
        for c in range(2):
            n = zs * 2 + c
            forward(n).wait_send()

            @pl.when(jnp.logical_not(stays(zs, c)))
            def _(n=n, zs=zs, c=c):
                for a in range(3):
                    out_copy(a, n, zs, c).wait_send()


def per_device(q, k, v, g, local_offsets, partner_pool, partner_picks):
    hbm = pl.BlockSpec(memory_space=pltpu.HBM)
    sm = pl.BlockSpec(memory_space=pltpu.SMEM)
    dma = pltpu.SemaphoreType.DMA
    i32 = jnp.int32
    return pl.pallas_call(
        kernel,
        name="butterfly",
        out_shape=tuple(jax.ShapeDtypeStruct((128, 2048), bf16) for _ in range(3)),
        in_specs=[hbm] * 6 + [sm],
        out_specs=(hbm, hbm, hbm),
        scratch_shapes=[
            pltpu.VMEM((16, 256, 256), bf16),
            pltpu.VMEM((32, 128, 256), bf16),
            pltpu.VMEM((32, 128, 128), bf16),
            pltpu.VMEM((ZERO + 1, 128, 256), bf16),
            pltpu.VMEM((NKEY * 128, 256), f32),
            pltpu.VMEM((NKEY * 128, 256), f32),
            pltpu.VMEM((16, 128, 128), bf16),
            pltpu.VMEM((10, 128, 256), f32),
            pltpu.VMEM((11, 128, 256), f32),
            pltpu.VMEM((11, 128, 256), f32),
            pltpu.VMEM((16, 128, 256), bf16),
            pltpu.VMEM((2, 4, 8), i32),
            pltpu.VMEM((2, 2, 4, 8), i32),
            pltpu.SMEM((2, 4, 8), i32),
            pltpu.SMEM((2, 2, 4, 8), i32),
            pltpu.SMEM((16 * NKEY,), i32),
            pltpu.SMEM((16 * TILES,), i32),
            dma((4, 16)),
            dma((4, 16)),
            dma((2, 16)),
            dma((2, 4)),
            dma((2,)),
            dma((3, 16)),
            dma((3, 16)),
            dma((2,)),
        ],
        compiler_params=pltpu.CompilerParams(
            collective_id=0, has_side_effects=True, vmem_limit_bytes=58 << 20
        ),
    )(q, k, v, g, local_offsets.T, partner_picks.transpose(1, 2, 0), partner_pool.transpose(2, 1, 0))


def solution(mesh):
    tok = P(("ctx", "head"), None)
    return jax.shard_map(
        per_device,
        mesh=mesh,
        in_specs=(tok, tok, tok, tok, P("ctx", None), P(), P("ctx", None, None)),
        out_specs=(tok, tok, tok),
        check_vma=False,
    )
```

```python
import jax
import jax.numpy as jnp
from jax import lax
from jax.experimental import pallas as pl
from jax.experimental.pallas import tpu as pltpu
from jax.sharding import PartitionSpec as P

MESH = pl.DeviceIdType.MESH
DH = 128
BLK = 128
NKEY = 12
TILES = 18
ZERO = 16 * NKEY
SCALE = DH**-0.5
f32 = jnp.float32
bf16 = jnp.bfloat16
SHIFTS = (0, 1, 7, 2, 6, 3, 5, 4)
ORDER = [(dx, dz) for dz in SHIFTS for dx in (0, 1)]


def place():
    ctx = lax.axis_index("ctx")
    head = lax.axis_index("head")
    return ctx, (ctx // 2) % 2, (ctx % 2) * 4 + head // 2, head % 2


def device(ctx, xb, z, core):
    return ((ctx // 4) * 4 + xb * 2 + z // 4, (z % 4) * 2 + core)


def remote(src, dst, ssem, rsem, dev):
    return pltpu.make_async_remote_copy(
        src_ref=src, dst_ref=dst, send_sem=ssem, recv_sem=rsem, device_id=dev, device_id_type=MESH
    )


def dot_t(a, b):
    return lax.dot_general(a, b, (((1,), (1,)), ((), ())), preferred_element_type=f32)


def dot(a, b):
    return jnp.dot(a, b, preferred_element_type=f32)


def tables(offs, picks, pool, group0, idx, slot):
    @pl.loop(0, 16)
    def _(n):
        u, i = n // 8, n % 8
        g = group0 + u
        loc = [(i + offs[u, j, i]) % 8 for j in range(4)]
        for j in range(4):
            idx[n * NKEY + j] = u * 8 + loc[j]
        for kb in range(8):
            s = jnp.int32(ZERO)
            for j in range(4):
                s = jnp.where(loc[j] == kb, n * NKEY + j, s)
            slot[n * TILES + kb] = s
        for b in range(2):
            base = (1 - u) * 8 if b == 0 else 16 + u * 8
            picked = [picks[u, b, t, i] for t in range(4)]
            for t in range(4):
                idx[n * NKEY + 4 + b * 4 + t] = base + pool[picked[t], b, g]
            for p in range(5):
                s = jnp.int32(ZERO)
                for t in range(4):
                    s = jnp.where(picked[t] == p, n * NKEY + 4 + b * 4 + t, s)
                slot[n * TILES + 8 + b * 5 + p] = s


def pool_place(pool, group, b, kb, none):
    s = jnp.int32(none)
    for p in range(5):
        s = jnp.where(pool[p, b, group] == kb, p, s)
    return s


def scores(n, idx, qd, kv, sp):
    rows = jnp.concatenate([kv[idx[n * NKEY + j]] for j in range(NKEY)], axis=0)
    sp[...] = dot_t(rows, qd[n])


def softmax_grads(n, sp, x):
    m = jnp.full((8, 128), -jnp.inf, f32)
    for j in range(NKEY):
        s = sp[j * 128 : (j + 1) * 128, 0:128].reshape(16, 8, 128)
        m = jnp.maximum(m, jnp.max(s, axis=0))
    m = jnp.max(m, axis=0, keepdims=True) * SCALE
    den = jnp.zeros((8, 128), f32)
    num = jnp.zeros((8, 128), f32)
    for j in range(NKEY):
        s = sp[j * 128 : (j + 1) * 128, 0:128]
        p = sp[j * 128 : (j + 1) * 128, 128:256]
        e = jnp.exp(s * SCALE - m)
        sp[j * 128 : (j + 1) * 128, 0:128] = e
        den = den + jnp.sum(e.reshape(16, 8, 128), axis=0)
        num = num + jnp.sum((e * p).reshape(16, 8, 128), axis=0)
    rden = 1.0 / jnp.sum(den, axis=0, keepdims=True)
    delta = jnp.sum(num, axis=0, keepdims=True) * rden
    rscaled = rden * SCALE
    for j in range(NKEY):
        e = sp[j * 128 : (j + 1) * 128, 0:128]
        p = sp[j * 128 : (j + 1) * 128, 128:256]
        x[n * NKEY + j, :, 128:256] = (e * rden).astype(bf16)
        x[n * NKEY + j, :, 0:128] = ((e * rscaled) * (p - delta)).astype(bf16)


def query_grad(n, idx, kv, x, dq):
    keys = jnp.concatenate([kv[idx[n * NKEY + j], :, 0:128] for j in range(NKEY)], axis=0)
    ds = jnp.concatenate([x[n * NKEY + j, :, 0:128] for j in range(NKEY)], axis=0)
    out = lax.dot_general(ds, keys, (((0,), (0,)), ((), ())), preferred_element_type=f32)
    dq[n] = out.astype(bf16)


def shift(o):
    return lax.rem(o, 2) * ((o + 1) // 2) + (1 - lax.rem(o, 2)) * lax.rem(8 - o // 2, 8)


def kernel(
    q, k, v, g, offsets, partner_picks, pool,
    oq, ok, ov,
    qd, kv, x, sp0, sp1, dq, part, near, own, recv, fin,
    voffs, vpicks, offs, picks, idx, slot,
    ssem, rsem, fsem, msem, lsem, osem, orsem, psem,
):
    ctx, xb, z, core = place()
    group0 = (ctx // 4) * 4 + core * 2
    away = core != xb
    at_home = core == xb
    here_dev = device(ctx, xb, z, 1 - core)
    barrier = pltpu.get_barrier_semaphore()
    for dz in SHIFTS[::-1]:
        zd = (z + dz) % 8
        targets = [(core, 1 - xb), (1 - core, xb), (core, xb)]
        for xd, cd in targets[: 3 if dz else 2]:
            pl.semaphore_signal(
                barrier, 1, device_id=device(ctx, xd, zd, cd), device_id_type=MESH
            )

    @pl.when(away)
    def _():
        pl.semaphore_signal(
            barrier, 1, device_id=device(ctx, core, z, xb), device_id_type=MESH
        )

    qd[:, 0:128, 128:256] = jnp.zeros((16, 128, 128), bf16)
    qd[:, 128:256, 0:128] = jnp.zeros((16, 128, 128), bf16)
    pl.semaphore_wait(barrier, 23 + away.astype(jnp.int32))

    mine = (z % 4) * 2 + core
    mrow = z // 4
    small = ((offsets, voffs, offs), (partner_picks, vpicks, picks))
    meta_here = jnp.logical_and(at_home, mine == z)
    for dx in (0, 1):
        for b, (src, dst, _) in enumerate(small):
            rc = remote(
                src, dst.at[mrow], msem.at[b, dx], msem.at[b, 2 + mrow],
                device(ctx, xb ^ dx, mine, xb),
            )
            if dx == 1:
                rc.start()
            else:

                @pl.when(jnp.logical_not(meta_here))
                def _(rc=rc):
                    rc.start()

                @pl.when(meta_here)
                def _(src=src, dst=dst, b=b):
                    pltpu.make_async_copy(src, dst.at[mrow], msem.at[b, 2 + mrow]).start()

    slot_here = z * 2 + core
    srcs = (k, v, q, g)

    def place_of(a, n):
        if a == 0:
            return kv.at[n, :, 0:128]
        if a == 1:
            return kv.at[n, :, 128:256]
        if a == 2:
            return qd.at[n, 0:128, 0:128]
        return qd.at[n, 128:256, 128:256]

    for a0 in (0, 2):
        for o, (dx, dz) in enumerate(ORDER):
            xd, zd = xb ^ dx, (z + dz) % 8
            cols = pl.ds(pl.multiple_of((xd * 8 + zd) * 128, 128), 128)
            for a in (a0, a0 + 1):
                src = srcs[a].at[:, cols]
                dst = place_of(a, slot_here)
                rc = remote(
                    src, dst, ssem.at[a, o], rsem.at[a, slot_here], device(ctx, xd, zd, xb)
                )
                if (dx, dz) == (0, 0):

                    @pl.when(away)
                    def _(rc=rc):
                        rc.start()

                    @pl.when(at_home)
                    def _(src=src, dst=dst, a=a):
                        pltpu.make_async_copy(src, dst, rsem.at[a, slot_here]).start()
                else:
                    rc.start()

    def arrived(a, n):
        ref = place_of(a, n)
        remote(ref, ref, ssem.at[a, 0], rsem.at[a, n], here_dev).wait_recv()

    for n in range(2):
        for b, (src, dst, _) in enumerate(small):
            remote(src, dst.at[n], msem.at[b, 0], msem.at[b, 2 + n], here_dev).wait_recv()
    for b, (_, src, dst) in enumerate(small):
        local = pltpu.make_async_copy(src, dst, lsem.at[b])
        local.start()
        local.wait()
    tables(offs, picks, pool, group0, idx, slot)
    x[ZERO] = jnp.zeros((128, 256), bf16)
    near[...] = jnp.zeros((11, 128, 256), f32)
    part[...] = jnp.zeros((10, 128, 256), f32)
    recv[10] = jnp.zeros((128, 256), f32)

    def forward(n):
        return remote(kv.at[n], kv.at[16 + n], fsem.at[0, n], fsem.at[1, n], here_dev)

    @pl.loop(0, 8)
    def _(o):
        zs = (z + 8 - shift(o)) % 8
        for c in range(2):
            n = zs * 2 + c
            arrived(0, n)
            arrived(1, n)
            forward(n).start()

    @pl.loop(0, 8)
    def _(o):
        zs = (z + 8 - shift(o)) % 8
        for c in range(2):
            forward(zs * 2 + c).wait_recv()

    cols = pl.ds(pl.multiple_of((xb * 8 + z) * 128, 128), 128)
    row = xb * 8 + z
    outs = (oq, ok, ov)

    def result(a, n):
        if a == 0:
            return dq.at[n]
        return fin.at[n, :, (a - 1) * 128 : a * 128]

    def out_copy(a, n, zs, c):
        return remote(
            result(a, n), outs[a].at[:, cols], osem.at[a, n], orsem.at[a, row],
            device(ctx, core, zs, c),
        )

    def stays(zs, c):
        return jnp.logical_and(at_home, jnp.logical_and(zs == z, core == c))

    def send(a, n, zs, c):
        @pl.when(jnp.logical_not(stays(zs, c)))
        def _():
            out_copy(a, n, zs, c).start()

        @pl.when(stays(zs, c))
        def _():
            pltpu.make_async_copy(result(a, n), outs[a].at[:, cols], orsem.at[a, row]).start()

    @pl.loop(0, 8)
    def _(o):
        zs = (z + 8 - shift(o)) % 8
        for c in range(2):
            arrived(2, zs * 2 + c)
            arrived(3, zs * 2 + c)
        a, b = zs * 2, zs * 2 + 1
        scores(a, idx, qd, kv, sp0)
        scores(b, idx, qd, kv, sp1)
        softmax_grads(a, sp0, x)
        query_grad(a, idx, kv, x, dq)
        softmax_grads(b, sp1, x)
        query_grad(b, idx, kv, x, dq)
        for c in range(2):
            send(0, zs * 2 + c, zs, c)
        u = zs // 4
        rows = [
            jnp.concatenate([x[slot[a * TILES + t]], x[slot[b * TILES + t]]], axis=1)
            for t in range(8, TILES)
        ]
        add = dot(jnp.concatenate(rows, axis=0), qd[pl.ds(a, 2)].reshape(512, 256))
        for t in range(5):
            near[u * 5 + t] += add[t * 128 : (t + 1) * 128]
            part[u * 5 + t] += add[(t + 5) * 128 : (t + 6) * 128]

    def tile_sum(u, t):
        rows = jnp.concatenate([x[slot[(u * 8 + i) * TILES + t]] for i in range(8)], axis=1)
        return dot(rows, qd[pl.ds(u * 8, 8)].reshape(2048, 256))

    swap = remote(part, recv.at[0:10], psem.at[0], psem.at[1], here_dev)
    swap.start()

    @pl.loop(0, 16)
    def _(n):
        own[n] = tile_sum(n // 8, n % 8)

    swap.wait()

    @pl.loop(0, 8)
    def _(o):
        zs = (z + 8 - shift(7 - o)) % 8
        u = zs // 4
        for c in range(2):
            n = zs * 2 + c
            p = (1 - u) * 5 + pool_place(pool, group0 + 1 - u, 0, n % 8, 10 - (1 - u) * 5)
            r = u * 5 + pool_place(
                pool, (ctx // 4) * 4 + (1 - core) * 2 + u, 1, n % 8, 10 - u * 5
            )
            fin[n] = (own[n] + near[p] + recv[r]).astype(bf16)
            send(1, n, zs, c)
            send(2, n, zs, c)

    @pl.loop(0, 16)
    def _(r):
        for a in range(3):
            ref = outs[a].at[:, pl.ds(pl.multiple_of(r * 128, 128), 128)]
            remote(ref, ref, osem.at[a, 0], orsem.at[a, r], here_dev).wait_recv()

    for o, (dx, dz) in enumerate(ORDER):
        for a in range(4):
            src = srcs[a].at[:, 0:128]
            rc = remote(src, src, ssem.at[a, o], rsem.at[a, 0], here_dev)
            if (dx, dz) == (0, 0):

                @pl.when(away)
                def _(rc=rc):
                    rc.wait_send()
            else:
                rc.wait_send()
    for b, (src, dst, _) in enumerate(small):
        remote(src, dst.at[0], msem.at[b, 1], msem.at[b, 2], here_dev).wait_send()

        @pl.when(jnp.logical_not(meta_here))
        def _(src=src, dst=dst, b=b):
            remote(src, dst.at[0], msem.at[b, 0], msem.at[b, 2], here_dev).wait_send()

    @pl.loop(0, 8)
    def _(zs):
        for c in range(2):
            n = zs * 2 + c
            forward(n).wait_send()

            @pl.when(jnp.logical_not(stays(zs, c)))
            def _(n=n, zs=zs, c=c):
                for a in range(3):
                    out_copy(a, n, zs, c).wait_send()


def per_device(q, k, v, g, local_offsets, partner_pool, partner_picks):
    hbm = pl.BlockSpec(memory_space=pltpu.HBM)
    sm = pl.BlockSpec(memory_space=pltpu.SMEM)
    dma = pltpu.SemaphoreType.DMA
    i32 = jnp.int32
    return pl.pallas_call(
        kernel,
        name="butterfly",
        out_shape=tuple(jax.ShapeDtypeStruct((128, 2048), bf16) for _ in range(3)),
        in_specs=[hbm] * 6 + [sm],
        out_specs=(hbm, hbm, hbm),
        scratch_shapes=[
            pltpu.VMEM((16, 256, 256), bf16),
            pltpu.VMEM((32, 128, 256), bf16),
            pltpu.VMEM((ZERO + 1, 128, 256), bf16),
            pltpu.VMEM((NKEY * 128, 256), f32),
            pltpu.VMEM((NKEY * 128, 256), f32),
            pltpu.VMEM((16, 128, 128), bf16),
            pltpu.VMEM((10, 128, 256), f32),
            pltpu.VMEM((11, 128, 256), f32),
            pltpu.VMEM((16, 128, 256), f32),
            pltpu.VMEM((11, 128, 256), f32),
            pltpu.VMEM((16, 128, 256), bf16),
            pltpu.VMEM((2, 4, 8), i32),
            pltpu.VMEM((2, 2, 4, 8), i32),
            pltpu.SMEM((2, 4, 8), i32),
            pltpu.SMEM((2, 2, 4, 8), i32),
            pltpu.SMEM((16 * NKEY,), i32),
            pltpu.SMEM((16 * TILES,), i32),
            dma((4, 16)),
            dma((4, 16)),
            dma((2, 16)),
            dma((2, 4)),
            dma((2,)),
            dma((3, 16)),
            dma((3, 16)),
            dma((2,)),
        ],
        compiler_params=pltpu.CompilerParams(
            collective_id=0, has_side_effects=True, vmem_limit_bytes=58 << 20
        ),
    )(q, k, v, g, local_offsets.T, partner_picks.transpose(1, 2, 0), partner_pool.transpose(2, 1, 0))


def solution(mesh):
    tok = P(("ctx", "head"), None)
    return jax.shard_map(
        per_device,
        mesh=mesh,
        in_specs=(tok, tok, tok, tok, P("ctx", None), P(), P("ctx", None, None)),
        out_specs=(tok, tok, tok),
        check_vma=False,
    )
```

```python
import jax
import jax.numpy as jnp
from jax import lax
from jax.experimental import pallas as pl
from jax.experimental.pallas import tpu as pltpu
from jax.sharding import PartitionSpec as P

MESH = pl.DeviceIdType.MESH
DH = 128
BLK = 128
NKEY = 12
TILES = 18
ZERO = 16 * NKEY
SCALE = DH**-0.5
f32 = jnp.float32
bf16 = jnp.bfloat16
SHIFTS = (0, 1, 7, 2, 6, 3, 5, 4)
ORDER = [(dx, dz) for dz in SHIFTS for dx in (0, 1)]


def place():
    ctx = lax.axis_index("ctx")
    head = lax.axis_index("head")
    return ctx, (ctx // 2) % 2, (ctx % 2) * 4 + head // 2, head % 2


def device(ctx, xb, z, core):
    return ((ctx // 4) * 4 + xb * 2 + z // 4, (z % 4) * 2 + core)


def remote(src, dst, ssem, rsem, dev):
    return pltpu.make_async_remote_copy(
        src_ref=src, dst_ref=dst, send_sem=ssem, recv_sem=rsem, device_id=dev, device_id_type=MESH
    )


def dot_t(a, b):
    return lax.dot_general(a, b, (((1,), (1,)), ((), ())), preferred_element_type=f32)


def dot(a, b):
    return jnp.dot(a, b, preferred_element_type=f32)


def tables(offs, picks, pool, group0, idx, slot):
    @pl.loop(0, 16)
    def _(n):
        u, i = n // 8, n % 8
        g = group0 + u
        loc = [(i + offs[u, j, i]) % 8 for j in range(4)]
        for j in range(4):
            idx[n * NKEY + j] = u * 8 + loc[j]
        for kb in range(8):
            s = jnp.int32(ZERO)
            for j in range(4):
                s = jnp.where(loc[j] == kb, n * NKEY + j, s)
            slot[n * TILES + kb] = s
        for b in range(2):
            base = (1 - u) * 8 if b == 0 else 16 + u * 8
            picked = [picks[u, b, t, i] for t in range(4)]
            for t in range(4):
                idx[n * NKEY + 4 + b * 4 + t] = base + pool[picked[t], b, g]
            for p in range(5):
                s = jnp.int32(ZERO)
                for t in range(4):
                    s = jnp.where(picked[t] == p, n * NKEY + 4 + b * 4 + t, s)
                slot[n * TILES + 8 + b * 5 + p] = s


def pool_place(pool, group, b, kb, none):
    s = jnp.int32(none)
    for p in range(5):
        s = jnp.where(pool[p, b, group] == kb, p, s)
    return s


def scores(n, idx, qd, kv, sp):
    rows = jnp.concatenate([kv[idx[n * NKEY + j]] for j in range(NKEY)], axis=0)
    sp[...] = dot_t(rows, qd[n])


def softmax_grads(n, sp, x):
    m = jnp.full((8, 128), -jnp.inf, f32)
    for j in range(NKEY):
        s = sp[j * 128 : (j + 1) * 128, 0:128].reshape(16, 8, 128)
        m = jnp.maximum(m, jnp.max(s, axis=0))
    m = jnp.max(m, axis=0, keepdims=True) * SCALE
    den = jnp.zeros((8, 128), f32)
    num = jnp.zeros((8, 128), f32)
    for j in range(NKEY):
        s = sp[j * 128 : (j + 1) * 128, 0:128]
        p = sp[j * 128 : (j + 1) * 128, 128:256]
        e = jnp.exp(s * SCALE - m)
        sp[j * 128 : (j + 1) * 128, 0:128] = e
        den = den + jnp.sum(e.reshape(16, 8, 128), axis=0)
        num = num + jnp.sum((e * p).reshape(16, 8, 128), axis=0)
    rden = 1.0 / jnp.sum(den, axis=0, keepdims=True)
    delta = jnp.sum(num, axis=0, keepdims=True) * rden
    rscaled = rden * SCALE
    for j in range(NKEY):
        e = sp[j * 128 : (j + 1) * 128, 0:128]
        p = sp[j * 128 : (j + 1) * 128, 128:256]
        x[n * NKEY + j, :, 128:256] = (e * rden).astype(bf16)
        x[n * NKEY + j, :, 0:128] = ((e * rscaled) * (p - delta)).astype(bf16)


def query_grad(n, idx, kv, x, dq):
    keys = jnp.concatenate([kv[idx[n * NKEY + j], :, 0:128] for j in range(NKEY)], axis=0)
    ds = jnp.concatenate([x[n * NKEY + j, :, 0:128] for j in range(NKEY)], axis=0)
    out = lax.dot_general(ds, keys, (((0,), (0,)), ((), ())), preferred_element_type=f32)
    dq[n] = out.astype(bf16)


def shift(o):
    return lax.rem(o, 2) * ((o + 1) // 2) + (1 - lax.rem(o, 2)) * lax.rem(8 - o // 2, 8)


def kernel(
    q, k, v, g, offsets, partner_picks, all_pools,
    oq, ok, ov,
    qd, kv, x, sp0, sp1, dq, part, near, own, part_half, recv, fin,
    voffs, vpicks, offs, picks, pool, idx, slot,
    ssem, rsem, fsem, msem, lsem, osem, orsem, psem,
):
    ctx, xb, z, core = place()
    group0 = (ctx // 4) * 4 + core * 2
    away = core != xb
    at_home = core == xb
    here_dev = device(ctx, xb, z, 1 - core)
    barrier = pltpu.get_barrier_semaphore()
    for dz in SHIFTS[::-1]:
        zd = (z + dz) % 8
        targets = [(core, 1 - xb), (1 - core, xb), (core, xb)]
        for xd, cd in targets[: 3 if dz else 2]:
            pl.semaphore_signal(
                barrier, 1, device_id=device(ctx, xd, zd, cd), device_id_type=MESH
            )

    @pl.when(away)
    def _():
        pl.semaphore_signal(
            barrier, 1, device_id=device(ctx, core, z, xb), device_id_type=MESH
        )

    pool_copy = pltpu.make_async_copy(all_pools, pool, lsem.at[2])
    pool_copy.start()
    qd[:, 0:128, 128:256] = jnp.zeros((16, 128, 128), bf16)
    qd[:, 128:256, 0:128] = jnp.zeros((16, 128, 128), bf16)
    pl.semaphore_wait(barrier, 23 + away.astype(jnp.int32))

    mine = (z % 4) * 2 + core
    mrow = z // 4
    small = ((offsets, voffs, offs), (partner_picks, vpicks, picks))
    meta_here = jnp.logical_and(at_home, mine == z)
    for dx in (0, 1):
        for b, (src, dst, _) in enumerate(small):
            rc = remote(
                src, dst.at[mrow], msem.at[b, dx], msem.at[b, 2 + mrow],
                device(ctx, xb ^ dx, mine, xb),
            )
            if dx == 1:
                rc.start()
            else:

                @pl.when(jnp.logical_not(meta_here))
                def _(rc=rc):
                    rc.start()

                @pl.when(meta_here)
                def _(src=src, dst=dst, b=b):
                    pltpu.make_async_copy(src, dst.at[mrow], msem.at[b, 2 + mrow]).start()

    slot_here = z * 2 + core
    srcs = (k, v, q, g)

    def place_of(a, n):
        if a == 0:
            return kv.at[n, :, 0:128]
        if a == 1:
            return kv.at[n, :, 128:256]
        if a == 2:
            return qd.at[n, 0:128, 0:128]
        return qd.at[n, 128:256, 128:256]

    for a0 in (0, 2):
        for o, (dx, dz) in enumerate(ORDER):
            xd, zd = xb ^ dx, (z + dz) % 8
            cols = pl.ds(pl.multiple_of((xd * 8 + zd) * 128, 128), 128)
            for a in (a0, a0 + 1):
                src = srcs[a].at[:, cols]
                dst = place_of(a, slot_here)
                rc = remote(
                    src, dst, ssem.at[a, o], rsem.at[a, slot_here], device(ctx, xd, zd, xb)
                )
                if (dx, dz) == (0, 0):

                    @pl.when(away)
                    def _(rc=rc):
                        rc.start()

                    @pl.when(at_home)
                    def _(src=src, dst=dst, a=a):
                        pltpu.make_async_copy(src, dst, rsem.at[a, slot_here]).start()
                else:
                    rc.start()

    def arrived(a, n):
        ref = place_of(a, n)
        remote(ref, ref, ssem.at[a, 0], rsem.at[a, n], here_dev).wait_recv()

    for n in range(2):
        for b, (src, dst, _) in enumerate(small):
            remote(src, dst.at[n], msem.at[b, 0], msem.at[b, 2 + n], here_dev).wait_recv()
    for b, (_, src, dst) in enumerate(small):
        local = pltpu.make_async_copy(src, dst, lsem.at[b])
        local.start()
        local.wait()
    pool_copy.wait()
    tables(offs, picks, pool, group0, idx, slot)
    x[ZERO] = jnp.zeros((128, 256), bf16)
    near[...] = jnp.zeros((11, 128, 256), f32)
    part[...] = jnp.zeros((10, 128, 256), f32)
    recv[10] = jnp.zeros((128, 256), bf16)

    def forward(n):
        return remote(kv.at[n], kv.at[16 + n], fsem.at[0, n], fsem.at[1, n], here_dev)

    @pl.loop(0, 8)
    def _(o):
        zs = (z + 8 - shift(o)) % 8
        for c in range(2):
            n = zs * 2 + c
            arrived(0, n)
            arrived(1, n)
            forward(n).start()

    @pl.loop(0, 8)
    def _(o):
        zs = (z + 8 - shift(o)) % 8
        for c in range(2):
            forward(zs * 2 + c).wait_recv()

    cols = pl.ds(pl.multiple_of((xb * 8 + z) * 128, 128), 128)
    row = xb * 8 + z
    outs = (oq, ok, ov)

    def result(a, n):
        if a == 0:
            return dq.at[n]
        return fin.at[n, :, (a - 1) * 128 : a * 128]

    def out_copy(a, n, zs, c):
        return remote(
            result(a, n), outs[a].at[:, cols], osem.at[a, n], orsem.at[a, row],
            device(ctx, core, zs, c),
        )

    def stays(zs, c):
        return jnp.logical_and(at_home, jnp.logical_and(zs == z, core == c))

    def send(a, n, zs, c):
        @pl.when(jnp.logical_not(stays(zs, c)))
        def _():
            out_copy(a, n, zs, c).start()

        @pl.when(stays(zs, c))
        def _():
            pltpu.make_async_copy(result(a, n), outs[a].at[:, cols], orsem.at[a, row]).start()

    def await_pair(zs):
        for c in range(2):
            arrived(2, zs * 2 + c)
            arrived(3, zs * 2 + c)

    def attend_pair(zs):
        a, b = zs * 2, zs * 2 + 1
        scores(a, idx, qd, kv, sp0)
        scores(b, idx, qd, kv, sp1)
        softmax_grads(a, sp0, x)
        query_grad(a, idx, kv, x, dq)
        softmax_grads(b, sp1, x)
        query_grad(b, idx, kv, x, dq)

    def add_pair(zs):
        a, b = zs * 2, zs * 2 + 1
        u = zs // 4
        rows = [
            jnp.concatenate([x[slot[a * TILES + t]], x[slot[b * TILES + t]]], axis=1)
            for t in range(8, TILES)
        ]
        add = dot(jnp.concatenate(rows, axis=0), qd[pl.ds(a, 2)].reshape(512, 256))
        for t in range(5):
            near[u * 5 + t] += add[t * 128 : (t + 1) * 128]
            part[u * 5 + t] += add[(t + 5) * 128 : (t + 6) * 128]

    def source(o):
        return (z + 8 - shift(o)) % 8

    @pl.loop(0, 7)
    def _(o):
        zs = source(o)
        await_pair(zs)
        attend_pair(zs)
        add_pair(zs)

    await_pair(source(7))

    @pl.loop(1, 8)
    def _(o):
        zs = source(7 - o)
        for c in range(2):
            send(0, zs * 2 + c, zs, c)

    attend_pair(source(7))
    for c in range(2):
        send(0, source(7) * 2 + c, source(7), c)
    add_pair(source(7))

    def tile_sum(u, t):
        rows = jnp.concatenate([x[slot[(u * 8 + i) * TILES + t]] for i in range(8)], axis=1)
        return dot(rows, qd[pl.ds(u * 8, 8)].reshape(2048, 256))

    part_half[...] = part[...].astype(bf16)
    swap = remote(part_half, recv.at[0:10], psem.at[0], psem.at[1], here_dev)
    swap.start()

    def finish(n, zs, c, local):
        u = zs // 4
        p = (1 - u) * 5 + pool_place(pool, group0 + 1 - u, 0, n % 8, 10 - (1 - u) * 5)
        r = u * 5 + pool_place(pool, (ctx // 4) * 4 + (1 - core) * 2 + u, 1, n % 8, 10 - u * 5)
        fin[n] = (local + near[p] + recv[r].astype(f32)).astype(bf16)
        send(1, n, zs, c)
        send(2, n, zs, c)

    @pl.loop(0, 4)
    def _(o):
        zs = source(7 - o)
        for c in range(2):
            n = zs * 2 + c
            own[n] = tile_sum(zs // 4, n % 8)

    swap.wait()

    @pl.loop(0, 4)
    def _(o):
        zs = source(7 - o)
        for c in range(2):
            n = zs * 2 + c
            finish(n, zs, c, own[n])

    @pl.loop(4, 8)
    def _(o):
        zs = source(7 - o)
        for c in range(2):
            n = zs * 2 + c
            finish(n, zs, c, tile_sum(zs // 4, n % 8))

    @pl.loop(0, 16)
    def _(r):
        for a in range(3):
            ref = outs[a].at[:, pl.ds(pl.multiple_of(r * 128, 128), 128)]
            remote(ref, ref, osem.at[a, 0], orsem.at[a, r], here_dev).wait_recv()

    for o, (dx, dz) in enumerate(ORDER):
        for a in range(4):
            src = srcs[a].at[:, 0:128]
            rc = remote(src, src, ssem.at[a, o], rsem.at[a, 0], here_dev)
            if (dx, dz) == (0, 0):

                @pl.when(away)
                def _(rc=rc):
                    rc.wait_send()
            else:
                rc.wait_send()
    for b, (src, dst, _) in enumerate(small):
        remote(src, dst.at[0], msem.at[b, 1], msem.at[b, 2], here_dev).wait_send()

        @pl.when(jnp.logical_not(meta_here))
        def _(src=src, dst=dst, b=b):
            remote(src, dst.at[0], msem.at[b, 0], msem.at[b, 2], here_dev).wait_send()

    @pl.loop(0, 8)
    def _(zs):
        for c in range(2):
            n = zs * 2 + c
            forward(n).wait_send()

            @pl.when(jnp.logical_not(stays(zs, c)))
            def _(n=n, zs=zs, c=c):
                for a in range(3):
                    out_copy(a, n, zs, c).wait_send()


PIECES = [(a, h) for h in range(2) for a in range(3)]


def copy_kernel(a, b, c, oa, ob, oc, buf, sem):
    srcs, dsts = (a, b, c), (oa, ob, oc)
    ins, outs = [], []
    for i, (r, h) in enumerate(PIECES):
        rows = pl.ds(h * 64, 64)
        ins.append(pltpu.make_async_copy(srcs[r].at[rows], buf.at[r, rows], sem.at[0, i]))
        outs.append(pltpu.make_async_copy(buf.at[r, rows], dsts[r].at[rows], sem.at[1, i]))
    for cp in ins:
        cp.start()
    for cp, out in zip(ins, outs):
        cp.wait()
        out.start()
    for cp in outs:
        cp.wait()


def per_device(q, k, v, g, local_offsets, partner_pool, partner_picks):
    hbm = pl.BlockSpec(memory_space=pltpu.HBM)
    dma = pltpu.SemaphoreType.DMA
    i32 = jnp.int32
    results = pl.pallas_call(
        kernel,
        name="butterfly",
        out_shape=tuple(jax.ShapeDtypeStruct((128, 2048), bf16) for _ in range(3)),
        in_specs=[hbm] * 7,
        out_specs=(hbm, hbm, hbm),
        scratch_shapes=[
            pltpu.VMEM((16, 256, 256), bf16),
            pltpu.VMEM((32, 128, 256), bf16),
            pltpu.VMEM((ZERO + 1, 128, 256), bf16),
            pltpu.VMEM((NKEY * 128, 256), f32),
            pltpu.VMEM((NKEY * 128, 256), f32),
            pltpu.VMEM((16, 128, 128), bf16),
            pltpu.VMEM((10, 128, 256), f32),
            pltpu.VMEM((11, 128, 256), f32),
            pltpu.VMEM((16, 128, 256), f32),
            pltpu.VMEM((10, 128, 256), bf16),
            pltpu.VMEM((11, 128, 256), bf16),
            pltpu.VMEM((16, 128, 256), bf16),
            pltpu.VMEM((2, 4, 8), i32),
            pltpu.VMEM((2, 2, 4, 8), i32),
            pltpu.SMEM((2, 4, 8), i32),
            pltpu.SMEM((2, 2, 4, 8), i32),
            pltpu.SMEM((5, 2, 32), i32),
            pltpu.SMEM((16 * NKEY,), i32),
            pltpu.SMEM((16 * TILES,), i32),
            dma((4, 16)),
            dma((4, 16)),
            dma((2, 16)),
            dma((2, 4)),
            dma((3,)),
            dma((3, 16)),
            dma((3, 16)),
            dma((2,)),
        ],
        compiler_params=pltpu.CompilerParams(
            collective_id=0, has_side_effects=True, vmem_limit_bytes=58 << 20
        ),
    )(q, k, v, g, local_offsets.T, partner_picks.transpose(1, 2, 0), partner_pool.transpose(2, 1, 0))
    return pl.pallas_call(
        copy_kernel,
        name="results",
        out_shape=tuple(jax.ShapeDtypeStruct((128, 2048), bf16) for _ in range(3)),
        in_specs=[hbm] * 3,
        out_specs=(hbm, hbm, hbm),
        scratch_shapes=[pltpu.VMEM((3, 128, 2048), bf16), dma((2, 6))],
        compiler_params=pltpu.CompilerParams(vmem_limit_bytes=58 << 20),
    )(*results)


def solution(mesh):
    tok = P(("ctx", "head"), None)
    return jax.shard_map(
        per_device,
        mesh=mesh,
        in_specs=(tok, tok, tok, tok, P("ctx", None), P(), P("ctx", None, None)),
        out_specs=(tok, tok, tok),
        check_vma=False,
    )
```

```python
import jax
import jax.numpy as jnp
from jax import lax
from jax.experimental import pallas as pl
from jax.experimental.pallas import tpu as pltpu
from jax.sharding import PartitionSpec as P

MESH = pl.DeviceIdType.MESH
DH = 128
BLK = 128
NKEY = 12
TILES = 18
ZERO = 16 * NKEY
SCALE = DH**-0.5
f32 = jnp.float32
bf16 = jnp.bfloat16
SHIFTS = (0, 1, 7, 2, 6, 3, 5, 4)
ORDER = [(dx, dz) for dz in SHIFTS for dx in (0, 1)]


def place():
    ctx = lax.axis_index("ctx")
    head = lax.axis_index("head")
    return ctx, (ctx // 2) % 2, (ctx % 2) * 4 + head // 2, head % 2


def device(ctx, xb, z, core):
    return ((ctx // 4) * 4 + xb * 2 + z // 4, (z % 4) * 2 + core)


def remote(src, dst, ssem, rsem, dev):
    return pltpu.make_async_remote_copy(
        src_ref=src, dst_ref=dst, send_sem=ssem, recv_sem=rsem, device_id=dev, device_id_type=MESH
    )


def dot_t(a, b):
    return lax.dot_general(a, b, (((1,), (1,)), ((), ())), preferred_element_type=f32)


def dot(a, b):
    return jnp.dot(a, b, preferred_element_type=f32)


def tables(offs, picks, pool, group0, idx, slot):
    @pl.loop(0, 16)
    def _(n):
        u, i = n // 8, n % 8
        g = group0 + u
        loc = [(i + offs[u, j, i]) % 8 for j in range(4)]
        for j in range(4):
            idx[n * NKEY + j] = u * 8 + loc[j]
        for kb in range(8):
            s = jnp.int32(ZERO)
            for j in range(4):
                s = jnp.where(loc[j] == kb, n * NKEY + j, s)
            slot[n * TILES + kb] = s
        for b in range(2):
            base = (1 - u) * 8 if b == 0 else 16 + u * 8
            picked = [picks[u, b, t, i] for t in range(4)]
            for t in range(4):
                idx[n * NKEY + 4 + b * 4 + t] = base + pool[picked[t], b, g]
            for p in range(5):
                s = jnp.int32(ZERO)
                for t in range(4):
                    s = jnp.where(picked[t] == p, n * NKEY + 4 + b * 4 + t, s)
                slot[n * TILES + 8 + b * 5 + p] = s


def pool_place(pool, group, b, kb, none):
    s = jnp.int32(none)
    for p in range(5):
        s = jnp.where(pool[p, b, group] == kb, p, s)
    return s


def scores(n, idx, qd, kv, sp):
    rows = jnp.concatenate([kv[idx[n * NKEY + j]] for j in range(NKEY)], axis=0)
    sp[...] = dot_t(rows, qd[n])


def softmax_grads(n, sp, x):
    m = jnp.full((8, 128), -jnp.inf, f32)
    for j in range(NKEY):
        s = sp[j * 128 : (j + 1) * 128, 0:128].reshape(16, 8, 128)
        m = jnp.maximum(m, jnp.max(s, axis=0))
    m = jnp.max(m, axis=0, keepdims=True) * SCALE
    den = jnp.zeros((8, 128), f32)
    num = jnp.zeros((8, 128), f32)
    for j in range(NKEY):
        s = sp[j * 128 : (j + 1) * 128, 0:128]
        p = sp[j * 128 : (j + 1) * 128, 128:256]
        e = jnp.exp(s * SCALE - m)
        sp[j * 128 : (j + 1) * 128, 0:128] = e
        den = den + jnp.sum(e.reshape(16, 8, 128), axis=0)
        num = num + jnp.sum((e * p).reshape(16, 8, 128), axis=0)
    rden = 1.0 / jnp.sum(den, axis=0, keepdims=True)
    delta = jnp.sum(num, axis=0, keepdims=True) * rden
    rscaled = rden * SCALE
    for j in range(NKEY):
        e = sp[j * 128 : (j + 1) * 128, 0:128]
        p = sp[j * 128 : (j + 1) * 128, 128:256]
        x[n * NKEY + j, :, 128:256] = (e * rden).astype(bf16)
        x[n * NKEY + j, :, 0:128] = ((e * rscaled) * (p - delta)).astype(bf16)


def query_grad(n, idx, kv, x, dq):
    keys = jnp.concatenate([kv[idx[n * NKEY + j], :, 0:128] for j in range(NKEY)], axis=0)
    ds = jnp.concatenate([x[n * NKEY + j, :, 0:128] for j in range(NKEY)], axis=0)
    out = lax.dot_general(ds, keys, (((0,), (0,)), ((), ())), preferred_element_type=f32)
    dq[n] = out.astype(bf16)


def shift(o):
    return lax.rem(o, 2) * ((o + 1) // 2) + (1 - lax.rem(o, 2)) * lax.rem(8 - o // 2, 8)


def kernel(
    q, k, v, g, offsets, partner_picks, all_pools,
    oq, ok, ov,
    qd, kv, x, sp0, sp1, dq, part, near, own, part_half, recv, fin,
    voffs, vpicks, offs, picks, pool, idx, slot,
    ssem, rsem, fsem, msem, lsem, osem, orsem, psem,
):
    ctx, xb, z, core = place()
    group0 = (ctx // 4) * 4 + core * 2
    away = core != xb
    at_home = core == xb
    here_dev = device(ctx, xb, z, 1 - core)
    barrier = pltpu.get_barrier_semaphore()
    for dz in SHIFTS[::-1]:
        zd = (z + dz) % 8
        targets = [(core, 1 - xb), (1 - core, xb), (core, xb)]
        for xd, cd in targets[: 3 if dz else 2]:
            pl.semaphore_signal(
                barrier, 1, device_id=device(ctx, xd, zd, cd), device_id_type=MESH
            )

    @pl.when(away)
    def _():
        pl.semaphore_signal(
            barrier, 1, device_id=device(ctx, core, z, xb), device_id_type=MESH
        )

    pool_copy = pltpu.make_async_copy(all_pools, pool, lsem.at[2])
    pool_copy.start()
    qd[:, 0:128, 128:256] = jnp.zeros((16, 128, 128), bf16)
    qd[:, 128:256, 0:128] = jnp.zeros((16, 128, 128), bf16)
    pl.semaphore_wait(barrier, 23 + away.astype(jnp.int32))

    mine = (z % 4) * 2 + core
    mrow = z // 4
    small = ((offsets, voffs, offs), (partner_picks, vpicks, picks))
    meta_here = jnp.logical_and(at_home, mine == z)
    for dx in (0, 1):
        for b, (src, dst, _) in enumerate(small):
            rc = remote(
                src, dst.at[mrow], msem.at[b, dx], msem.at[b, 2 + mrow],
                device(ctx, xb ^ dx, mine, xb),
            )
            if dx == 1:
                rc.start()
            else:

                @pl.when(jnp.logical_not(meta_here))
                def _(rc=rc):
                    rc.start()

                @pl.when(meta_here)
                def _(src=src, dst=dst, b=b):
                    pltpu.make_async_copy(src, dst.at[mrow], msem.at[b, 2 + mrow]).start()

    slot_here = z * 2 + core
    srcs = (k, v, q, g)

    def place_of(a, n):
        if a == 0:
            return kv.at[n, :, 0:128]
        if a == 1:
            return kv.at[n, :, 128:256]
        if a == 2:
            return qd.at[n, 0:128, 0:128]
        return qd.at[n, 128:256, 128:256]

    for a0 in (0, 2):
        for o, (dx, dz) in enumerate(ORDER):
            xd, zd = xb ^ dx, (z + dz) % 8
            cols = pl.ds(pl.multiple_of((xd * 8 + zd) * 128, 128), 128)
            for a in (a0, a0 + 1):
                src = srcs[a].at[:, cols]
                dst = place_of(a, slot_here)
                rc = remote(
                    src, dst, ssem.at[a, o], rsem.at[a, slot_here], device(ctx, xd, zd, xb)
                )
                if (dx, dz) == (0, 0):

                    @pl.when(away)
                    def _(rc=rc):
                        rc.start()

                    @pl.when(at_home)
                    def _(src=src, dst=dst, a=a):
                        pltpu.make_async_copy(src, dst, rsem.at[a, slot_here]).start()
                else:
                    rc.start()

    def arrived(a, n):
        ref = place_of(a, n)
        remote(ref, ref, ssem.at[a, 0], rsem.at[a, n], here_dev).wait_recv()

    for n in range(2):
        for b, (src, dst, _) in enumerate(small):
            remote(src, dst.at[n], msem.at[b, 0], msem.at[b, 2 + n], here_dev).wait_recv()
    for b, (_, src, dst) in enumerate(small):
        local = pltpu.make_async_copy(src, dst, lsem.at[b])
        local.start()
        local.wait()
    pool_copy.wait()
    tables(offs, picks, pool, group0, idx, slot)
    x[ZERO] = jnp.zeros((128, 256), bf16)
    near[...] = jnp.zeros((11, 128, 256), f32)
    part[...] = jnp.zeros((10, 128, 256), f32)
    recv[10] = jnp.zeros((128, 256), bf16)

    def forward(n):
        return remote(kv.at[n], kv.at[16 + n], fsem.at[0, n], fsem.at[1, n], here_dev)

    @pl.loop(0, 8)
    def _(o):
        zs = (z + 8 - shift(o)) % 8
        for c in range(2):
            n = zs * 2 + c
            arrived(0, n)
            arrived(1, n)
            forward(n).start()

    @pl.loop(0, 8)
    def _(o):
        zs = (z + 8 - shift(o)) % 8
        for c in range(2):
            forward(zs * 2 + c).wait_recv()

    cols = pl.ds(pl.multiple_of((xb * 8 + z) * 128, 128), 128)
    row = xb * 8 + z
    outs = (oq, ok, ov)

    def result(a, n):
        if a == 0:
            return dq.at[n]
        return fin.at[n, :, (a - 1) * 128 : a * 128]

    def out_copy(a, n, zs, c):
        return remote(
            result(a, n), outs[a].at[:, cols], osem.at[a, n], orsem.at[a, row],
            device(ctx, core, zs, c),
        )

    def stays(zs, c):
        return jnp.logical_and(at_home, jnp.logical_and(zs == z, core == c))

    def send(a, n, zs, c):
        @pl.when(jnp.logical_not(stays(zs, c)))
        def _():
            out_copy(a, n, zs, c).start()

        @pl.when(stays(zs, c))
        def _():
            pltpu.make_async_copy(result(a, n), outs[a].at[:, cols], orsem.at[a, row]).start()

    def await_pair(zs):
        for c in range(2):
            arrived(2, zs * 2 + c)
            arrived(3, zs * 2 + c)

    def attend_pair(zs):
        a, b = zs * 2, zs * 2 + 1
        scores(a, idx, qd, kv, sp0)
        scores(b, idx, qd, kv, sp1)
        softmax_grads(a, sp0, x)
        query_grad(a, idx, kv, x, dq)
        softmax_grads(b, sp1, x)
        query_grad(b, idx, kv, x, dq)

    def add_pair(zs):
        a, b = zs * 2, zs * 2 + 1
        u = zs // 4
        rows = [
            jnp.concatenate([x[slot[a * TILES + t]], x[slot[b * TILES + t]]], axis=1)
            for t in range(8, TILES)
        ]
        add = dot(jnp.concatenate(rows, axis=0), qd[pl.ds(a, 2)].reshape(512, 256))
        for t in range(5):
            near[u * 5 + t] += add[t * 128 : (t + 1) * 128]
            part[u * 5 + t] += add[(t + 5) * 128 : (t + 6) * 128]

    def source(o):
        return (z + 8 - shift(o)) % 8

    @pl.loop(0, 8)
    def _(o):
        zs = source(o)
        await_pair(zs)
        attend_pair(zs)
        for c in range(2):
            send(0, zs * 2 + c, zs, c)
        add_pair(zs)

    def tile_sum(u, t):
        rows = jnp.concatenate([x[slot[(u * 8 + i) * TILES + t]] for i in range(8)], axis=1)
        return dot(rows, qd[pl.ds(u * 8, 8)].reshape(2048, 256))

    part_half[...] = part[...].astype(bf16)
    swap = remote(part_half, recv.at[0:10], psem.at[0], psem.at[1], here_dev)
    swap.start()

    def finish(n, zs, c, local):
        u = zs // 4
        p = (1 - u) * 5 + pool_place(pool, group0 + 1 - u, 0, n % 8, 10 - (1 - u) * 5)
        r = u * 5 + pool_place(pool, (ctx // 4) * 4 + (1 - core) * 2 + u, 1, n % 8, 10 - u * 5)
        fin[n] = (local + near[p] + recv[r].astype(f32)).astype(bf16)
        send(1, n, zs, c)
        send(2, n, zs, c)

    @pl.loop(0, 4)
    def _(o):
        zs = source(7 - o)
        for c in range(2):
            n = zs * 2 + c
            own[n] = tile_sum(zs // 4, n % 8)

    swap.wait()

    @pl.loop(0, 4)
    def _(o):
        zs = source(7 - o)
        for c in range(2):
            n = zs * 2 + c
            finish(n, zs, c, own[n])

    @pl.loop(4, 8)
    def _(o):
        zs = source(7 - o)
        for c in range(2):
            n = zs * 2 + c
            finish(n, zs, c, tile_sum(zs // 4, n % 8))

    @pl.loop(0, 16)
    def _(r):
        for a in range(3):
            ref = outs[a].at[:, pl.ds(pl.multiple_of(r * 128, 128), 128)]
            remote(ref, ref, osem.at[a, 0], orsem.at[a, r], here_dev).wait_recv()

    for o, (dx, dz) in enumerate(ORDER):
        for a in range(4):
            src = srcs[a].at[:, 0:128]
            rc = remote(src, src, ssem.at[a, o], rsem.at[a, 0], here_dev)
            if (dx, dz) == (0, 0):

                @pl.when(away)
                def _(rc=rc):
                    rc.wait_send()
            else:
                rc.wait_send()
    for b, (src, dst, _) in enumerate(small):
        remote(src, dst.at[0], msem.at[b, 1], msem.at[b, 2], here_dev).wait_send()

        @pl.when(jnp.logical_not(meta_here))
        def _(src=src, dst=dst, b=b):
            remote(src, dst.at[0], msem.at[b, 0], msem.at[b, 2], here_dev).wait_send()

    @pl.loop(0, 8)
    def _(zs):
        for c in range(2):
            n = zs * 2 + c
            forward(n).wait_send()

            @pl.when(jnp.logical_not(stays(zs, c)))
            def _(n=n, zs=zs, c=c):
                for a in range(3):
                    out_copy(a, n, zs, c).wait_send()


PIECES = [(a, h) for h in range(2) for a in range(3)]


def copy_kernel(a, b, c, oa, ob, oc, buf, sem):
    srcs, dsts = (a, b, c), (oa, ob, oc)
    ins, outs = [], []
    for i, (r, h) in enumerate(PIECES):
        rows = pl.ds(h * 64, 64)
        ins.append(pltpu.make_async_copy(srcs[r].at[rows], buf.at[r, rows], sem.at[0, i]))
        outs.append(pltpu.make_async_copy(buf.at[r, rows], dsts[r].at[rows], sem.at[1, i]))
    for cp in ins:
        cp.start()
    for cp, out in zip(ins, outs):
        cp.wait()
        out.start()
    for cp in outs:
        cp.wait()


def per_device(q, k, v, g, local_offsets, partner_pool, partner_picks):
    hbm = pl.BlockSpec(memory_space=pltpu.HBM)
    dma = pltpu.SemaphoreType.DMA
    i32 = jnp.int32
    results = pl.pallas_call(
        kernel,
        name="butterfly",
        out_shape=tuple(jax.ShapeDtypeStruct((128, 2048), bf16) for _ in range(3)),
        in_specs=[hbm] * 7,
        out_specs=(hbm, hbm, hbm),
        scratch_shapes=[
            pltpu.VMEM((16, 256, 256), bf16),
            pltpu.VMEM((32, 128, 256), bf16),
            pltpu.VMEM((ZERO + 1, 128, 256), bf16),
            pltpu.VMEM((NKEY * 128, 256), f32),
            pltpu.VMEM((NKEY * 128, 256), f32),
            pltpu.VMEM((16, 128, 128), bf16),
            pltpu.VMEM((10, 128, 256), f32),
            pltpu.VMEM((11, 128, 256), f32),
            pltpu.VMEM((16, 128, 256), f32),
            pltpu.VMEM((10, 128, 256), bf16),
            pltpu.VMEM((11, 128, 256), bf16),
            pltpu.VMEM((16, 128, 256), bf16),
            pltpu.VMEM((2, 4, 8), i32),
            pltpu.VMEM((2, 2, 4, 8), i32),
            pltpu.SMEM((2, 4, 8), i32),
            pltpu.SMEM((2, 2, 4, 8), i32),
            pltpu.SMEM((5, 2, 32), i32),
            pltpu.SMEM((16 * NKEY,), i32),
            pltpu.SMEM((16 * TILES,), i32),
            dma((4, 16)),
            dma((4, 16)),
            dma((2, 16)),
            dma((2, 4)),
            dma((3,)),
            dma((3, 16)),
            dma((3, 16)),
            dma((2,)),
        ],
        compiler_params=pltpu.CompilerParams(
            collective_id=0, has_side_effects=True, vmem_limit_bytes=58 << 20
        ),
    )(q, k, v, g, local_offsets.T, partner_picks.transpose(1, 2, 0), partner_pool.transpose(2, 1, 0))
    return pl.pallas_call(
        copy_kernel,
        name="results",
        out_shape=tuple(jax.ShapeDtypeStruct((128, 2048), bf16) for _ in range(3)),
        in_specs=[hbm] * 3,
        out_specs=(hbm, hbm, hbm),
        scratch_shapes=[pltpu.VMEM((3, 128, 2048), bf16), dma((2, 6))],
        compiler_params=pltpu.CompilerParams(vmem_limit_bytes=58 << 20),
    )(*results)


def solution(mesh):
    tok = P(("ctx", "head"), None)
    return jax.shard_map(
        per_device,
        mesh=mesh,
        in_specs=(tok, tok, tok, tok, P("ctx", None), P(), P("ctx", None, None)),
        out_specs=(tok, tok, tok),
        check_vma=False,
    )
```

```python
import jax
import jax.numpy as jnp
from jax import lax
from jax.experimental import pallas as pl
from jax.experimental.pallas import tpu as pltpu
from jax.sharding import PartitionSpec as P

MESH = pl.DeviceIdType.MESH
DH = 128
BLK = 128
NKEY = 12
TILES = 18
ZERO = 16 * NKEY
SCALE = DH**-0.5
f32 = jnp.float32
bf16 = jnp.bfloat16
SHIFTS = (0, 1, 7, 2, 6, 3, 5, 4)
ORDER = [(dx, dz) for dz in SHIFTS for dx in (0, 1)]


def place():
    ctx = lax.axis_index("ctx")
    head = lax.axis_index("head")
    return ctx, (ctx // 2) % 2, (ctx % 2) * 4 + head // 2, head % 2


def device(ctx, xb, z, core):
    return ((ctx // 4) * 4 + xb * 2 + z // 4, (z % 4) * 2 + core)


def remote(src, dst, ssem, rsem, dev):
    return pltpu.make_async_remote_copy(
        src_ref=src, dst_ref=dst, send_sem=ssem, recv_sem=rsem, device_id=dev, device_id_type=MESH
    )


def dot_t(a, b):
    return lax.dot_general(a, b, (((1,), (1,)), ((), ())), preferred_element_type=f32)


def dot(a, b):
    return jnp.dot(a, b, preferred_element_type=f32)


def tables(offs, picks, pool, group0, idx, slot):
    @pl.loop(0, 16)
    def _(n):
        u, i = n // 8, n % 8
        g = group0 + u
        loc = [(i + offs[u, j, i]) % 8 for j in range(4)]
        for j in range(4):
            idx[n * NKEY + j] = u * 8 + loc[j]
        for kb in range(8):
            s = jnp.int32(ZERO)
            for j in range(4):
                s = jnp.where(loc[j] == kb, n * NKEY + j, s)
            slot[n * TILES + kb] = s
        for b in range(2):
            base = (1 - u) * 8 if b == 0 else 16 + u * 8
            picked = [picks[u, b, t, i] for t in range(4)]
            for t in range(4):
                idx[n * NKEY + 4 + b * 4 + t] = base + pool[picked[t], b, g]
            for p in range(5):
                s = jnp.int32(ZERO)
                for t in range(4):
                    s = jnp.where(picked[t] == p, n * NKEY + 4 + b * 4 + t, s)
                slot[n * TILES + 8 + b * 5 + p] = s


def pool_place(pool, group, b, kb, none):
    s = jnp.int32(none)
    for p in range(5):
        s = jnp.where(pool[p, b, group] == kb, p, s)
    return s


def scores(n, idx, qd, kv, sp):
    rows = jnp.concatenate([kv[idx[n * NKEY + j]] for j in range(NKEY)], axis=0)
    sp[...] = dot_t(rows, qd[n])


def softmax_grads(n, sp, x):
    m = jnp.full((8, 128), -jnp.inf, f32)
    for j in range(NKEY):
        s = sp[j * 128 : (j + 1) * 128, 0:128].reshape(16, 8, 128)
        m = jnp.maximum(m, jnp.max(s, axis=0))
    m = jnp.max(m, axis=0, keepdims=True) * SCALE
    den = jnp.zeros((8, 128), f32)
    num = jnp.zeros((8, 128), f32)
    for j in range(NKEY):
        s = sp[j * 128 : (j + 1) * 128, 0:128]
        p = sp[j * 128 : (j + 1) * 128, 128:256]
        e = jnp.exp(s * SCALE - m)
        sp[j * 128 : (j + 1) * 128, 0:128] = e
        den = den + jnp.sum(e.reshape(16, 8, 128), axis=0)
        num = num + jnp.sum((e * p).reshape(16, 8, 128), axis=0)
    rden = 1.0 / jnp.sum(den, axis=0, keepdims=True)
    delta = jnp.sum(num, axis=0, keepdims=True) * rden
    rscaled = rden * SCALE
    for j in range(NKEY):
        e = sp[j * 128 : (j + 1) * 128, 0:128]
        p = sp[j * 128 : (j + 1) * 128, 128:256]
        x[n * NKEY + j, :, 128:256] = (e * rden).astype(bf16)
        x[n * NKEY + j, :, 0:128] = ((e * rscaled) * (p - delta)).astype(bf16)


def query_grad(n, idx, kv, x, dq):
    keys = jnp.concatenate([kv[idx[n * NKEY + j], :, 0:128] for j in range(NKEY)], axis=0)
    ds = jnp.concatenate([x[n * NKEY + j, :, 0:128] for j in range(NKEY)], axis=0)
    out = lax.dot_general(ds, keys, (((0,), (0,)), ((), ())), preferred_element_type=f32)
    dq[n] = out.astype(bf16)


def shift(o):
    return lax.rem(o, 2) * ((o + 1) // 2) + (1 - lax.rem(o, 2)) * lax.rem(8 - o // 2, 8)


def kernel(
    q, k, v, g, offsets, partner_picks, all_pools,
    oq, ok, ov,
    qd, kv, x, sp0, sp1, dq, part, near, own, part_half, recv, fin,
    voffs, vpicks, offs, picks, pool, idx, slot,
    ssem, rsem, fsem, msem, lsem, osem, orsem, psem,
):
    ctx, xb, z, core = place()
    group0 = (ctx // 4) * 4 + core * 2
    away = core != xb
    at_home = core == xb
    here_dev = device(ctx, xb, z, 1 - core)
    barrier = pltpu.get_barrier_semaphore()
    for dz in SHIFTS[::-1]:
        zd = (z + dz) % 8
        targets = [(core, 1 - xb), (1 - core, xb), (core, xb)]
        for xd, cd in targets[: 3 if dz else 2]:
            pl.semaphore_signal(
                barrier, 1, device_id=device(ctx, xd, zd, cd), device_id_type=MESH
            )

    @pl.when(away)
    def _():
        pl.semaphore_signal(
            barrier, 1, device_id=device(ctx, core, z, xb), device_id_type=MESH
        )

    pool_copy = pltpu.make_async_copy(all_pools, pool, lsem.at[2])
    pool_copy.start()
    qd[:, 0:128, 128:256] = jnp.zeros((16, 128, 128), bf16)
    qd[:, 128:256, 0:128] = jnp.zeros((16, 128, 128), bf16)
    pl.semaphore_wait(barrier, 23 + away.astype(jnp.int32))

    mine = (z % 4) * 2 + core
    mrow = z // 4
    small = ((offsets, voffs, offs), (partner_picks, vpicks, picks))
    meta_here = jnp.logical_and(at_home, mine == z)
    for dx in (0, 1):
        for b, (src, dst, _) in enumerate(small):
            rc = remote(
                src, dst.at[mrow], msem.at[b, dx], msem.at[b, 2 + mrow],
                device(ctx, xb ^ dx, mine, xb),
            )
            if dx == 1:
                rc.start()
            else:

                @pl.when(jnp.logical_not(meta_here))
                def _(rc=rc):
                    rc.start()

                @pl.when(meta_here)
                def _(src=src, dst=dst, b=b):
                    pltpu.make_async_copy(src, dst.at[mrow], msem.at[b, 2 + mrow]).start()

    slot_here = z * 2 + core
    srcs = (k, v, q, g)

    def place_of(a, n):
        if a == 0:
            return kv.at[n, :, 0:128]
        if a == 1:
            return kv.at[n, :, 128:256]
        if a == 2:
            return qd.at[n, 0:128, 0:128]
        return qd.at[n, 128:256, 128:256]

    for a0 in (0, 2):
        for o, (dx, dz) in enumerate(ORDER):
            xd, zd = xb ^ dx, (z + dz) % 8
            cols = pl.ds(pl.multiple_of((xd * 8 + zd) * 128, 128), 128)
            for a in (a0, a0 + 1):
                src = srcs[a].at[:, cols]
                dst = place_of(a, slot_here)
                rc = remote(
                    src, dst, ssem.at[a, o], rsem.at[a, slot_here], device(ctx, xd, zd, xb)
                )
                if (dx, dz) == (0, 0):

                    @pl.when(away)
                    def _(rc=rc):
                        rc.start()

                    @pl.when(at_home)
                    def _(src=src, dst=dst, a=a):
                        pltpu.make_async_copy(src, dst, rsem.at[a, slot_here]).start()
                else:
                    rc.start()

    def arrived(a, n):
        ref = place_of(a, n)
        remote(ref, ref, ssem.at[a, 0], rsem.at[a, n], here_dev).wait_recv()

    for n in range(2):
        for b, (src, dst, _) in enumerate(small):
            remote(src, dst.at[n], msem.at[b, 0], msem.at[b, 2 + n], here_dev).wait_recv()
    for b, (_, src, dst) in enumerate(small):
        local = pltpu.make_async_copy(src, dst, lsem.at[b])
        local.start()
        local.wait()
    pool_copy.wait()
    tables(offs, picks, pool, group0, idx, slot)
    x[ZERO] = jnp.zeros((128, 256), bf16)
    near[...] = jnp.zeros((11, 128, 256), f32)
    part[...] = jnp.zeros((10, 128, 256), f32)
    recv[10] = jnp.zeros((128, 256), bf16)

    def forward(n):
        return remote(kv.at[n], kv.at[16 + n], fsem.at[0, n], fsem.at[1, n], here_dev)

    @pl.loop(0, 8)
    def _(o):
        zs = (z + 8 - shift(o)) % 8
        for c in range(2):
            n = zs * 2 + c
            arrived(0, n)
            arrived(1, n)
            forward(n).start()

    @pl.loop(0, 8)
    def _(o):
        zs = (z + 8 - shift(o)) % 8
        for c in range(2):
            forward(zs * 2 + c).wait_recv()

    cols = pl.ds(pl.multiple_of((xb * 8 + z) * 128, 128), 128)
    row = xb * 8 + z
    outs = (oq, ok, ov)

    def result(a, n):
        if a == 0:
            return dq.at[n]
        return fin.at[n, :, (a - 1) * 128 : a * 128]

    def out_copy(a, n, zs, c):
        return remote(
            result(a, n), outs[a].at[:, cols], osem.at[a, n], orsem.at[a, row],
            device(ctx, core, zs, c),
        )

    def stays(zs, c):
        return jnp.logical_and(at_home, jnp.logical_and(zs == z, core == c))

    def send(a, n, zs, c):
        @pl.when(jnp.logical_not(stays(zs, c)))
        def _():
            out_copy(a, n, zs, c).start()

        @pl.when(stays(zs, c))
        def _():
            pltpu.make_async_copy(result(a, n), outs[a].at[:, cols], orsem.at[a, row]).start()

    def await_pair(zs):
        for c in range(2):
            arrived(2, zs * 2 + c)
            arrived(3, zs * 2 + c)

    def attend_pair(zs):
        a, b = zs * 2, zs * 2 + 1
        scores(a, idx, qd, kv, sp0)
        scores(b, idx, qd, kv, sp1)
        softmax_grads(a, sp0, x)
        query_grad(a, idx, kv, x, dq)
        softmax_grads(b, sp1, x)
        query_grad(b, idx, kv, x, dq)

    def add_pair(zs):
        a, b = zs * 2, zs * 2 + 1
        u = zs // 4
        rows = [
            jnp.concatenate([x[slot[a * TILES + t]], x[slot[b * TILES + t]]], axis=1)
            for t in range(8, TILES)
        ]
        add = dot(jnp.concatenate(rows, axis=0), qd[pl.ds(a, 2)].reshape(512, 256))
        for t in range(5):
            near[u * 5 + t] += add[t * 128 : (t + 1) * 128]
            part[u * 5 + t] += add[(t + 5) * 128 : (t + 6) * 128]

    def swap_half(u):
        rows = pl.ds(u * 5, 5)
        return remote(
            part_half.at[rows], recv.at[rows], psem.at[0, u], psem.at[1, u], here_dev
        )

    def start_swap(u):
        rows = pl.ds(u * 5, 5)
        part_half[rows] = part[rows].astype(bf16)
        swap_half(u).start()

    def source(o):
        return (z + 8 - shift(o)) % 8

    @pl.loop(0, 8)
    def _(o):
        zs = source(o)
        await_pair(zs)

        @pl.when(o == 7)
        def _():
            start_swap(1 - zs // 4)

        attend_pair(zs)
        for c in range(2):
            send(0, zs * 2 + c, zs, c)
        add_pair(zs)

    def tile_sum(u, t):
        rows = jnp.concatenate([x[slot[(u * 8 + i) * TILES + t]] for i in range(8)], axis=1)
        return dot(rows, qd[pl.ds(u * 8, 8)].reshape(2048, 256))

    start_swap(source(7) // 4)

    def finish(n, zs, c, local):
        u = zs // 4
        p = (1 - u) * 5 + pool_place(pool, group0 + 1 - u, 0, n % 8, 10 - (1 - u) * 5)
        r = u * 5 + pool_place(pool, (ctx // 4) * 4 + (1 - core) * 2 + u, 1, n % 8, 10 - u * 5)
        fin[n] = (local + near[p] + recv[r].astype(f32)).astype(bf16)
        send(1, n, zs, c)
        send(2, n, zs, c)

    @pl.loop(0, 3)
    def _(o):
        zs = source(7 - o)
        for c in range(2):
            n = zs * 2 + c
            own[n] = tile_sum(zs // 4, n % 8)

    swap_half(0).wait()
    swap_half(1).wait()

    @pl.loop(0, 3)
    def _(o):
        zs = source(7 - o)
        for c in range(2):
            n = zs * 2 + c
            finish(n, zs, c, own[n])

    @pl.loop(3, 8)
    def _(o):
        zs = source(7 - o)
        for c in range(2):
            n = zs * 2 + c
            finish(n, zs, c, tile_sum(zs // 4, n % 8))

    @pl.loop(0, 16)
    def _(r):
        for a in range(3):
            ref = outs[a].at[:, pl.ds(pl.multiple_of(r * 128, 128), 128)]
            remote(ref, ref, osem.at[a, 0], orsem.at[a, r], here_dev).wait_recv()

    for o, (dx, dz) in enumerate(ORDER):
        for a in range(4):
            src = srcs[a].at[:, 0:128]
            rc = remote(src, src, ssem.at[a, o], rsem.at[a, 0], here_dev)
            if (dx, dz) == (0, 0):

                @pl.when(away)
                def _(rc=rc):
                    rc.wait_send()
            else:
                rc.wait_send()
    for b, (src, dst, _) in enumerate(small):
        remote(src, dst.at[0], msem.at[b, 1], msem.at[b, 2], here_dev).wait_send()

        @pl.when(jnp.logical_not(meta_here))
        def _(src=src, dst=dst, b=b):
            remote(src, dst.at[0], msem.at[b, 0], msem.at[b, 2], here_dev).wait_send()

    @pl.loop(0, 8)
    def _(zs):
        for c in range(2):
            n = zs * 2 + c
            forward(n).wait_send()

            @pl.when(jnp.logical_not(stays(zs, c)))
            def _(n=n, zs=zs, c=c):
                for a in range(3):
                    out_copy(a, n, zs, c).wait_send()


PIECES = [(a, h) for h in range(2) for a in range(3)]


def copy_kernel(a, b, c, oa, ob, oc, buf, sem):
    srcs, dsts = (a, b, c), (oa, ob, oc)
    ins, outs = [], []
    for i, (r, h) in enumerate(PIECES):
        rows = pl.ds(h * 64, 64)
        ins.append(pltpu.make_async_copy(srcs[r].at[rows], buf.at[r, rows], sem.at[0, i]))
        outs.append(pltpu.make_async_copy(buf.at[r, rows], dsts[r].at[rows], sem.at[1, i]))
    for cp in ins:
        cp.start()
    for cp, out in zip(ins, outs):
        cp.wait()
        out.start()
    for cp in outs:
        cp.wait()


def per_device(q, k, v, g, local_offsets, partner_pool, partner_picks):
    hbm = pl.BlockSpec(memory_space=pltpu.HBM)
    dma = pltpu.SemaphoreType.DMA
    i32 = jnp.int32
    results = pl.pallas_call(
        kernel,
        name="butterfly",
        out_shape=tuple(jax.ShapeDtypeStruct((128, 2048), bf16) for _ in range(3)),
        in_specs=[hbm] * 7,
        out_specs=(hbm, hbm, hbm),
        scratch_shapes=[
            pltpu.VMEM((16, 256, 256), bf16),
            pltpu.VMEM((32, 128, 256), bf16),
            pltpu.VMEM((ZERO + 1, 128, 256), bf16),
            pltpu.VMEM((NKEY * 128, 256), f32),
            pltpu.VMEM((NKEY * 128, 256), f32),
            pltpu.VMEM((16, 128, 128), bf16),
            pltpu.VMEM((10, 128, 256), f32),
            pltpu.VMEM((11, 128, 256), f32),
            pltpu.VMEM((16, 128, 256), f32),
            pltpu.VMEM((10, 128, 256), bf16),
            pltpu.VMEM((11, 128, 256), bf16),
            pltpu.VMEM((16, 128, 256), bf16),
            pltpu.VMEM((2, 4, 8), i32),
            pltpu.VMEM((2, 2, 4, 8), i32),
            pltpu.SMEM((2, 4, 8), i32),
            pltpu.SMEM((2, 2, 4, 8), i32),
            pltpu.SMEM((5, 2, 32), i32),
            pltpu.SMEM((16 * NKEY,), i32),
            pltpu.SMEM((16 * TILES,), i32),
            dma((4, 16)),
            dma((4, 16)),
            dma((2, 16)),
            dma((2, 4)),
            dma((3,)),
            dma((3, 16)),
            dma((3, 16)),
            dma((2, 2)),
        ],
        compiler_params=pltpu.CompilerParams(
            collective_id=0, has_side_effects=True, vmem_limit_bytes=58 << 20
        ),
    )(q, k, v, g, local_offsets.T, partner_picks.transpose(1, 2, 0), partner_pool.transpose(2, 1, 0))
    return pl.pallas_call(
        copy_kernel,
        name="results",
        out_shape=tuple(jax.ShapeDtypeStruct((128, 2048), bf16) for _ in range(3)),
        in_specs=[hbm] * 3,
        out_specs=(hbm, hbm, hbm),
        scratch_shapes=[pltpu.VMEM((3, 128, 2048), bf16), dma((2, 6))],
        compiler_params=pltpu.CompilerParams(vmem_limit_bytes=58 << 20),
    )(*results)


def solution(mesh):
    tok = P(("ctx", "head"), None)
    return jax.shard_map(
        per_device,
        mesh=mesh,
        in_specs=(tok, tok, tok, tok, P("ctx", None), P(), P("ctx", None, None)),
        out_specs=(tok, tok, tok),
        check_vma=False,
    )
```
